32 devices in a mesh: fourier: 8 (over z, y), elem: 4 (over x, core).
Axes of the slice: x: 2, y: 2, z: 4, core: 2. Of those that a mesh axis runs over, the one named last changes fastest.
Arguments:
- velocity: float32 [3, 528, 15552], P(None, 'fourier', 'elem'), may hold values from -0.4 to 0.4
- metric: float32 [4, 15552], P(None, 'elem'), may hold values from -5 to 5
- mass_weights: float32 [15552], P('elem'), may hold values from 0.2 to 2
Outputs:
- convective: float32 [3, 528, 15552], P(None, 'fourier', 'elem')
The draws below stay inside these ranges and needn't reach their ends.
All inputs are finite; a program needn't handle non-finite values.
Results may differ from the reference program's by a relative error of at most 0.0001.
Values sent between devices are 32-bit elements; how exact they have to be, the bound alone decides.
No kernel may reach another device: no remote copies, remote signals or barrier semaphores. Data moves between devices by JAX's collectives and lax.ppermute only.
A program may use at most 64 MiB of HBM per device.

```python
import math
import jax
import jax.numpy as jnp
import numpy as np
from jax import lax

NP = 9
NZ = 528
EDEV = 48
NODES = 15552
N_ELEM = 4


def shard_levels(own_key, extent, shards, least, high):
    level, own = 1.0, jax.random.fold_in(own_key, 6)
    for position, parts in shards:
        steps = jnp.exp(jax.random.uniform(jax.random.fold_in(own, position), (parts,), jnp.float32, least / len(shards), high / len(shards)))
        level = level * jnp.repeat(steps, extent[position] // parts).reshape([-1 if axis == position else 1 for axis in range(len(extent))])
    return level


def centred(key, dims, scale, bound, shards=(), kind=jnp.bfloat16):
    values = scale * jax.random.normal(key, dims, jnp.float32)
    if shards:
        values = values * shard_levels(key, dims, shards, -0.22, 0.18)
    return jnp.clip(values, -bound, bound).astype(kind)


def setup_inputs(seed: int = 0) -> dict:
    key_list = jax.random.split(jax.random.key(seed), 4)
    velocity = centred(key_list[0], (3, NZ, NODES), 0.06, 0.4, ((1, 8), (2, 4)), jnp.float32)
    metric = centred(key_list[1], (4, NODES), 1.0, 5.0, ((1, 4),), jnp.float32)
    mass_weights = jnp.clip(jnp.exp(math.log(2.0) - 2.3025851 * jax.random.uniform(key_list[2], (NODES,), jnp.float32) ** shard_levels(key_list[2], (NODES,), ((0, 4),), -0.2, 0.2)), 0.2, 2.0)
    return {"velocity": velocity, "metric": metric, "mass_weights": mass_weights}


HIGH = lax.Precision.HIGHEST


def gll_diff():
    gll_nodes = np.array([-1.0, -0.8997579954114602, -0.6771862795107377, -0.3631174638261782, 0.0, 0.3631174638261782, 0.6771862795107377, 0.8997579954114602, 1.0])
    points = gll_nodes.shape[0]
    bary_weight = np.ones(points)
    for i in range(points):
        for j in range(points):
            if i != j:
                bary_weight[i] = bary_weight[i] / (gll_nodes[i] - gll_nodes[j])
    matrix = np.zeros((points, points))
    for i in range(points):
        for j in range(points):
            if i != j:
                matrix[i, j] = bary_weight[j] / bary_weight[i] / (gll_nodes[i] - gll_nodes[j])
    for i in range(points):
        matrix[i, i] = -np.sum(matrix[i])
    return jnp.asarray(matrix, dtype=jnp.float32)


def fourier_tables(planes):
    plane_index = jnp.arange(planes, dtype=jnp.int32)
    wave_number = (plane_index + 1) // 2
    phase_index = (wave_number[:, None] * plane_index[None, :]) % planes
    angles = phase_index.astype(jnp.float32) * (2.0 * np.pi / planes)
    cosine_rows = (plane_index % 2 == 1) | (plane_index == 0)
    synthesis = jnp.where(cosine_rows[:, None], jnp.cos(angles), jnp.sin(angles))
    rate_factor = wave_number.astype(jnp.float32) * (8.0 / planes)
    rate_factor = jnp.where(plane_index == planes - 1, jnp.float32(0.0), rate_factor)
    spanwise_table = jnp.where(cosine_rows[:, None], -rate_factor[:, None] * jnp.sin(angles), rate_factor[:, None] * jnp.cos(angles))
    edge_rows = (plane_index == 0) | (plane_index == planes - 1)
    scale_rows = jnp.where(edge_rows, jnp.float32(1.0), jnp.float32(2.0)) / planes
    analysis = synthesis * scale_rows[:, None]
    return synthesis, spanwise_table, analysis


def convect(coeffs, factors, weights, slopes, synthesis, spanwise_table, per_row):
    planes = synthesis.shape[1]
    values = jnp.einsum('cmn,mz->czn', coeffs, synthesis, precision=HIGH)
    along_z = jnp.einsum('cmn,mz->czn', coeffs, spanwise_table, precision=HIGH)
    blocks = values.reshape(3, planes, per_row, NP, NP)
    along_xi = jnp.einsum('czeaj,bj->czeab', blocks, slopes, precision=HIGH).reshape(3, planes, per_row * NP * NP)
    along_eta = jnp.einsum('czejb,aj->czeab', blocks, slopes, precision=HIGH).reshape(3, planes, per_row * NP * NP)
    grad_x = factors[0] * along_xi + factors[2] * along_eta
    grad_y = factors[1] * along_xi + factors[3] * along_eta
    convective = values[0] * grad_x + values[1] * grad_y + values[2] * along_z
    return weights * convective


def x_assemble(coeffs, per_row):
    blocks = coeffs.reshape(coeffs.shape[0], coeffs.shape[1], per_row, NP, NP)
    shared = blocks[:, :, :-1, :, NP - 1] + blocks[:, :, 1:, :, 0]
    blocks = blocks.at[:, :, :-1, :, NP - 1].set(shared).at[:, :, 1:, :, 0].set(shared)
    return blocks.reshape(coeffs.shape)


def reference(velocity, metric, mass_weights):
    slopes = gll_diff()
    synthesis, spanwise_table, analysis = fourier_tables(NZ)
    row_nodes = EDEV * NP * NP

    def one_row(row_index, result):
        offset = (row_index * row_nodes).astype(jnp.int32)
        coeffs = lax.dynamic_slice_in_dim(velocity, offset, row_nodes, 2)
        factors = lax.dynamic_slice_in_dim(metric, offset, row_nodes, 1)
        weights = lax.dynamic_slice_in_dim(mass_weights, offset, row_nodes, 0)
        weighted = convect(coeffs, factors, weights, slopes, synthesis, spanwise_table, EDEV)
        summed = jnp.einsum('czn,mz->cmn', weighted, analysis, precision=HIGH)
        summed = x_assemble(summed, EDEV)
        return lax.dynamic_update_slice_in_dim(result, summed, offset, 2)

    result = jnp.zeros((3, NZ, NODES), jnp.float32)
    result = lax.fori_loop(0, N_ELEM, one_row, result)
    blocks = result.reshape(3, NZ, N_ELEM, EDEV, NP, NP)
    upper_rim = blocks[:, :, :, :, NP - 1]
    lower_rim = blocks[:, :, :, :, 0]
    zeros_rim = jnp.zeros_like(upper_rim[:, :, :1])
    from_below = jnp.concatenate([zeros_rim, upper_rim[:, :, :-1]], axis=2)
    from_above = jnp.concatenate([lower_rim[:, :, 1:], zeros_rim], axis=2)
    blocks = blocks.at[:, :, :, :, 0].add(from_below).at[:, :, :, :, NP - 1].add(from_above)
    return blocks.reshape(3, NZ, NODES)
```

```python
import functools

import jax
import jax.numpy as jnp
import ml_dtypes
import numpy as np
from jax import lax
from jax.experimental import pallas as pl
from jax.experimental.pallas import tpu as pltpu
from jax.sharding import PartitionSpec as P

NP = 9
HIGH = lax.Precision.HIGHEST
BF = jnp.bfloat16
F32 = jnp.float32
LANES = 256
CHUNKS = 2
VMEM_LIMIT = 40 << 20


def gll_diff():
    half = [0.3631174638261782, 0.6771862795107377, 0.8997579954114602, 1.0]
    nodes = np.array([-v for v in half[::-1]] + [0.0] + half)
    points = nodes.shape[0]
    gaps = nodes[:, None] - nodes[None, :] + np.eye(points)
    bary = 1.0 / np.prod(gaps, axis=1)
    matrix = bary[None, :] / bary[:, None] / gaps
    matrix[np.arange(points), np.arange(points)] = 0.0
    matrix[np.arange(points), np.arange(points)] = -matrix.sum(axis=1)
    return matrix


def fourier_tables(planes):
    index = np.arange(planes)
    wave = (index + 1) // 2
    angles = 2.0 * np.pi * ((wave[:, None] * index[None, :]) % planes) / planes
    cosine_rows = ((index % 2 == 1) | (index == 0))[:, None]
    synthesis = np.where(cosine_rows, np.cos(angles), np.sin(angles))
    rate = wave * (8.0 / planes)
    rate[planes - 1] = 0.0
    spanwise = np.where(cosine_rows, -rate[:, None] * np.sin(angles), rate[:, None] * np.cos(angles))
    scale = np.where((index == 0) | (index == planes - 1), 1.0, 2.0) / planes
    analysis = synthesis * scale[:, None]
    return synthesis, spanwise, analysis


def halves(table):
    table = np.asarray(table, np.float32)
    high = table.astype(ml_dtypes.bfloat16)
    low = (table - high.astype(np.float32)).astype(ml_dtypes.bfloat16)
    return high, low


class Plan:
    def __init__(self, count, modes, nodes):
        self.count, self.modes, self.nodes = count, modes, nodes
        self.planes = count * modes
        self.elements = nodes // (NP * NP)
        self.main = modes // 16 * 16
        self.left = modes - self.main
        self.per_piece = self.elements // (count * CHUNKS)
        self.width = self.per_piece * NP * NP
        self.columns = self.per_piece * (NP - 1) + 1
        self.rows = 3 * self.main + 8
        self.pieces = CHUNKS * count
        self.fits = (
            self.main > 0
            and 3 * self.left <= 8
            and self.elements % (count * CHUNKS) == 0
            and self.per_piece > 0
            and self.width <= LANES
            and self.columns <= 32
            and self.planes % 16 == 0
        )

    def lane(self, a, column):
        if column == 0:
            return a
        if column == self.columns - 1:
            return NP + a
        return 2 * NP + a * (self.columns - 2) + column - 1

    def tables(self):
        synthesis, spanwise, analysis = fourier_tables(self.planes)
        source = np.arange(self.count)
        main = (source[:, None] * self.modes + np.arange(self.main)[None, :]).reshape(-1)
        both = []
        for table in (synthesis, spanwise):
            high, low = halves(table.T[:, main])
            both.append(np.concatenate([high, high, low], axis=1))
        forward = np.stack(both)
        forward_left = np.zeros((3, 2, self.planes, 3 * 8 * self.count), ml_dtypes.bfloat16)
        back_left = np.zeros((3, 8 * self.count, 3 * self.planes), ml_dtypes.bfloat16)
        for c in range(3):
            for kind, table in enumerate((synthesis, spanwise)):
                wide = np.zeros((self.planes, 8 * self.count))
                for s in range(self.count):
                    for r in range(self.left):
                        wide[:, 8 * s + self.left * c + r] = table[s * self.modes + self.main + r]
                high, low = halves(wide)
                forward_left[c, kind] = np.concatenate([high, high, low], axis=1)
            tall = np.zeros((8 * self.count, self.planes))
            for s in range(self.count):
                for r in range(self.left):
                    tall[8 * s + self.left * c + r] = analysis[s * self.modes + self.main + r]
            high, low = halves(tall)
            back_left[c] = np.concatenate([high, high, low], axis=1)
        high, low = halves(analysis[main])
        back = np.concatenate([high, high, low], axis=1)
        return forward, forward_left, back, back_left

    def slopes(self):
        slopes = gll_diff()
        eye_elem, eye_side = np.eye(self.per_piece), np.eye(NP)
        wide = np.zeros((LANES, 2 * LANES))
        wide[: self.width, : self.width] = np.kron(eye_elem, np.kron(eye_side, slopes.T))
        wide[: self.width, LANES : LANES + self.width] = np.kron(eye_elem, np.kron(slopes.T, eye_side))
        high, low = halves(wide)
        return np.concatenate([high, high, low], axis=0)

    def assembly(self):
        join = np.zeros((3, LANES, 2 * LANES))
        rims = np.zeros((3, LANES, LANES))
        expand = np.zeros((LANES, LANES))
        for e in range(self.per_piece):
            for a in range(NP):
                for b in range(NP):
                    node, column = (e * NP + a) * NP + b, e * (NP - 1) + b
                    lane = self.lane(a, column)
                    expand[lane, node] = 1.0
                    for c in range(3):
                        join[c, node, lane] = 1.0
                        if a == 0:
                            join[c, node, LANES + 32 * c + column] = 1.0
                        if a == NP - 1:
                            join[c, node, LANES + 128 + 32 * c + column] = 1.0
        for c in range(3):
            for column in range(self.columns):
                rims[c, 32 * c + column, self.lane(0, column)] = 1.0
                rims[c, 128 + 32 * c + column, self.lane(NP - 1, column)] = 1.0
        kind = ml_dtypes.bfloat16
        join, rims, expand = join.astype(kind), rims.astype(kind), expand.astype(kind)
        return (
            np.concatenate([join, join], axis=1),
            np.concatenate([rims, rims], axis=1),
            np.concatenate([expand, expand], axis=0),
        )


def split(x):
    high = x.astype(BF)
    low = (x - high.astype(F32)).astype(BF)
    return high, low


def dot(a, b):
    return jnp.dot(a, b, preferred_element_type=F32)


def pack_kernel(plan, chunk, to_ref, v_ref, *refs):
    outs, buf = refs[:-1], refs[-1]
    lanes = lax.broadcasted_iota(jnp.int32, (1, LANES), 1)
    keep = lanes < plan.width
    for j in range(plan.count):
        start = (chunk * plan.count + j) * plan.width
        base = start // 128 * 128
        shift = start - base
        wide = LANES + 128
        tails = []
        for c in range(3):
            x = v_ref[c, : plan.main, base : base + wide]
            x = pltpu.roll(x, wide - shift, 1) if shift else x
            buf[j, plan.main * c : plan.main * (c + 1), :] = jnp.where(keep, x[:, :LANES], 0.0)
            if plan.left:
                tails.append(v_ref[c, plan.main : plan.modes, base : base + wide])
        tails.append(jnp.zeros((8 - 3 * plan.left, wide), F32))
        x = jnp.concatenate(tails, axis=0)
        x = pltpu.roll(x, wide - shift, 1) if shift else x
        buf[j, 3 * plan.main :, :] = jnp.where(keep, x[:, :LANES], 0.0)
    for s in range(plan.count):
        outs[s][...] = buf[to_ref[s]]


def synth_kernel(plan, from_ref, *refs):
    count, main = plan.count, plan.main
    blocks = refs[:count]
    t_ref, tl_ref, d_ref, join_ref, f_ref = refs[count : count + 5]
    w_ref, low_ref, up_ref = refs[count + 5 : count + 8]
    v3, raw, l3, u, dz = refs[count + 8 :]
    deep = main * count
    for s in range(count):
        source = from_ref[s]
        at = pl.multiple_of(source * main, main)
        for c in range(3):
            high, low = split(blocks[s][main * c : main * (c + 1), :])
            v3[c, pl.ds(at, main), :] = high
            v3[c, pl.ds(pl.multiple_of(deep + at, 16), main), :] = low
            v3[c, pl.ds(pl.multiple_of(2 * deep + at, 16), main), :] = high
        raw[pl.ds(pl.multiple_of(source * 8, 8), 8), :] = blocks[s][3 * main :, :]
    high, low = split(raw[...])
    l3[...] = jnp.concatenate([high, low, high], axis=0)

    @pl.loop(0, 3)
    def _(c):
        u[c] = dot(t_ref[0], v3[c]) + dot(tl_ref[c, 0], l3[...])
        dz[c] = dot(t_ref[1], v3[c]) + dot(tl_ref[c, 1], l3[...])

    low_ref[...] = jnp.zeros_like(low_ref)
    up_ref[...] = jnp.zeros_like(up_ref)

    @pl.loop(0, 3)
    def _(c):
        high, low = split(u[c])
        slope = dot(jnp.concatenate([high, low, high], axis=1), d_ref[...])
        along_xi, along_eta = slope[:, :LANES], slope[:, LANES:]
        grad_x = f_ref[0:1, :] * along_xi + f_ref[2:3, :] * along_eta
        grad_y = f_ref[1:2, :] * along_xi + f_ref[3:4, :] * along_eta
        weighted = f_ref[4:5, :] * (u[0] * grad_x + u[1] * grad_y + u[2] * dz[c])
        high, low = split(weighted)
        joined = dot(jnp.concatenate([high, low], axis=1), join_ref[c])
        w_ref[c] = joined[:, :LANES]
        low_ref[...] += joined[:, LANES : LANES + 128]
        up_ref[...] += joined[:, LANES + 128 :]


def analyse_kernel(plan, to_ref, w_ref, below_ref, above_ref, a_ref, al_ref, rims_ref, *refs):
    outs, buf, w3, tail = refs[:-3], refs[-3], refs[-2], refs[-1]
    count, main = plan.count, plan.main
    high, low = split(jnp.concatenate([below_ref[...], above_ref[...]], axis=1))
    rims = jnp.concatenate([high, low], axis=1)
    tail[...] = jnp.zeros_like(tail)

    @pl.loop(0, 3)
    def _(c):
        high, low = split(w_ref[c] + dot(rims, rims_ref[c]))
        w3[...] = jnp.concatenate([high, low, high], axis=0)
        coeffs = dot(a_ref[...], w3[...])
        for d in range(count):
            buf[d, pl.ds(pl.multiple_of(c * main, main), main), :] = coeffs[main * d : main * (d + 1)]
        tail[...] += dot(al_ref[c], w3[...])

    for d in range(count):
        buf[d, 3 * main :, :] = tail[8 * d : 8 * (d + 1), :]
    for s in range(count):
        outs[s][...] = buf[to_ref[s]]


def unpack_kernel(plan, from_ref, *refs):
    pieces, count = plan.pieces, plan.count
    blocks, e_ref, out_ref, held, total = refs[:pieces], refs[pieces], refs[pieces + 1], refs[pieces + 2], refs[pieces + 3]
    held[0] = jnp.zeros(held.shape[1:], F32)
    held[pieces + 1] = jnp.zeros(held.shape[1:], F32)
    for q in range(CHUNKS):
        for s in range(count):
            held[q * count + from_ref[s] + 1] = blocks[q * count + s][...]
    total[...] = jnp.zeros_like(total)
    lanes = lax.broadcasted_iota(jnp.int32, (1, 128), 1)

    @pl.loop(0, pieces)
    def _(i):
        before = held[i, :, :128]
        after = held[i + 2, :, :128]
        first = held[i + 1, :, :128]
        first = first + jnp.where(lanes < NP, pltpu.roll(before, 128 - NP, 1), 0.0)
        first = first + jnp.where((lanes >= NP) & (lanes < 2 * NP), pltpu.roll(after, NP, 1), 0.0)
        x = jnp.concatenate([first, held[i + 1, :, 128:]], axis=1)
        high, low = split(x)
        y = dot(jnp.concatenate([high, low], axis=1), e_ref[...])
        y = jnp.concatenate([y, jnp.zeros((plan.rows, 128), F32)], axis=1)
        start = i * plan.width
        base = pl.multiple_of(start // 128 * 128, 128)
        y = pltpu.roll(y, start - base, 1)
        total[:, pl.ds(base, LANES + 128)] += y

    for c in range(3):
        out_ref[c, : plan.main, :] = total[plan.main * c : plan.main * (c + 1), : plan.nodes]
        if plan.left:
            at = 3 * plan.main + plan.left * c
            out_ref[c, plan.main :, :] = total[at : at + plan.left, : plan.nodes]


def smem():
    return pl.BlockSpec(memory_space=pltpu.SMEM)


def vmem():
    return pl.BlockSpec(memory_space=pltpu.VMEM)


def params():
    return pltpu.CompilerParams(vmem_limit_bytes=VMEM_LIMIT)


def cost(flops, size):
    return pl.CostEstimate(flops=int(flops), bytes_accessed=int(size), transcendentals=0)


def pack(plan, chunk, to, velocity):
    span = -(-plan.nodes // 128) * 128
    reach = span
    if chunk == 0:
        last = (plan.count - 1) * plan.width
        reach = min(span, last // 128 * 128 + LANES + 128)
    block = jax.ShapeDtypeStruct((plan.rows, LANES), F32)
    return pl.pallas_call(
        functools.partial(pack_kernel, plan, chunk),
        grid=(1,),
        in_specs=[smem(), pl.BlockSpec((3, plan.modes, reach), lambda i: (0, 0, 0))],
        out_specs=[pl.BlockSpec((plan.rows, LANES), lambda i: (0, 0))] * plan.count,
        out_shape=[block] * plan.count,
        scratch_shapes=[pltpu.VMEM((plan.count, plan.rows, LANES), F32)],
        compiler_params=params(),
        cost_estimate=cost(0, 8 * plan.count * plan.rows * LANES),
        name=f"pack{chunk}",
    )(to, velocity)


def synth(plan, chunk, came, blocks, tables, factors):
    deep = plan.main * plan.count
    small = 8 * plan.count
    field = jax.ShapeDtypeStruct((3, plan.planes, LANES), F32)
    rim = jax.ShapeDtypeStruct((plan.planes, 128), F32)
    return pl.pallas_call(
        functools.partial(synth_kernel, plan),
        in_specs=[smem()] + [vmem()] * (plan.count + 5),
        out_specs=[vmem()] * 3,
        out_shape=[field, rim, rim],
        scratch_shapes=[
            pltpu.VMEM((3, 3 * deep, LANES), BF),
            pltpu.VMEM((small, LANES), F32),
            pltpu.VMEM((3 * small, LANES), BF),
            pltpu.VMEM((3, plan.planes, LANES), F32),
            pltpu.VMEM((3, plan.planes, LANES), F32),
        ],
        compiler_params=params(),
        cost_estimate=cost(3 * 2 * plan.planes * LANES * (6 * deep + 6 * LANES + 4 * LANES), 12 << 20),
        name=f"synth{chunk}",
    )(came, *blocks, *tables, factors)


def analyse(plan, chunk, to, field, below, above, tables):
    small = 8 * plan.count
    block = jax.ShapeDtypeStruct((plan.rows, LANES), F32)
    return pl.pallas_call(
        functools.partial(analyse_kernel, plan),
        in_specs=[smem()] + [vmem()] * 6,
        out_specs=[vmem()] * plan.count,
        out_shape=[block] * plan.count,
        scratch_shapes=[
            pltpu.VMEM((plan.count, plan.rows, LANES), F32),
            pltpu.VMEM((3 * plan.planes, LANES), BF),
            pltpu.VMEM((small, LANES), F32),
        ],
        compiler_params=params(),
        cost_estimate=cost(3 * 2 * plan.planes * LANES * 3 * plan.planes, 6 << 20),
        name=f"analyse{chunk}",
    )(to, field, below, above, *tables)


def unpack(plan, came, blocks, expand):
    span = -(-plan.nodes // 128) * 128
    whole = max(span, (plan.pieces - 1) * plan.width // 128 * 128 + LANES + 128)
    return pl.pallas_call(
        functools.partial(unpack_kernel, plan),
        in_specs=[smem()] + [vmem()] * (plan.pieces + 1),
        out_specs=vmem(),
        out_shape=jax.ShapeDtypeStruct((3, plan.modes, plan.nodes), F32),
        scratch_shapes=[
            pltpu.VMEM((plan.pieces + 2, plan.rows, LANES), F32),
            pltpu.VMEM((plan.rows, whole), F32),
        ],
        compiler_params=params(),
        cost_estimate=cost(2 * plan.pieces * plan.rows * LANES * 2 * LANES, 8 << 20),
        name="unpack",
    )(came, *blocks, expand)


def exchange(blocks, count):
    outs = [blocks[0]]
    for s in range(1, count):
        outs.append(lax.ppermute(blocks[s], "fourier", [(k, (k + s) % count) for k in range(count)]))
    return outs


def rim_exchange(low, up):
    ends = lax.axis_size("elem") - 1
    below = lax.ppermute(up, "elem", [(i, i + 1) for i in range(ends)])
    above = lax.ppermute(low, "elem", [(i + 1, i) for i in range(ends)])
    return below, above


def chunked(plan, velocity, metric, mass_weights):
    count = plan.count
    here = lax.axis_index("fourier").astype(jnp.int32)
    steps = jnp.arange(count, dtype=jnp.int32)
    to, came = (here + steps) % count, (here - steps + count) % count
    forward, forward_left, back, back_left = (jnp.asarray(t) for t in plan.tables())
    slopes = jnp.asarray(plan.slopes())
    join, rims, expand = (jnp.asarray(t) for t in plan.assembly())
    local = jnp.concatenate([metric, mass_weights[None], jnp.zeros((3, plan.nodes), F32)], axis=0)

    spread = [exchange(pack(plan, q, to, velocity), count) for q in range(CHUNKS)]
    returned = []
    for q in range(CHUNKS):
        start = (here + q * count) * plan.width
        factors = lax.dynamic_slice_in_dim(local, start, plan.width, 1)
        factors = jnp.pad(factors, ((0, 0), (0, LANES - plan.width)))
        field, low, up = synth(plan, q, came, spread[q], (forward, forward_left, slopes, join), factors)
        below, above = rim_exchange(low, up)
        returned += exchange(analyse(plan, q, to, field, below, above, (back, back_left, rims)), count)
    return unpack(plan, came, returned, expand)


def add_shifted(field, source, reach, side):
    count = field.shape[-1]
    node = np.arange(count)
    keep = side(node) & (node + reach >= 0) & (node + reach < count)
    pads = [(0, 0)] * (field.ndim - 1)
    if reach > 0:
        moved = jnp.pad(source[..., reach:], pads + [(0, reach)])
    else:
        moved = jnp.pad(source[..., :reach], pads + [(-reach, 0)])
    return field + jnp.where(jnp.asarray(keep), moved, 0.0)


def plain(plan, velocity, metric, mass_weights):
    count, square = plan.count, NP * NP
    synthesis, spanwise, analysis = (jnp.asarray(t, F32) for t in fourier_tables(plan.planes))
    slopes = gll_diff()
    group = plan.elements // count
    eye_elem, eye_side = np.eye(group), np.eye(NP)
    xi_matrix = jnp.asarray(np.kron(eye_elem, np.kron(eye_side, slopes.T)), F32)
    eta_matrix = jnp.asarray(np.kron(eye_elem, np.kron(slopes.T, eye_side)), F32)
    spread = lax.all_to_all(velocity, "fourier", split_axis=2, concat_axis=1, tiled=True)
    offset = lax.axis_index("fourier") * group * square
    factors = lax.dynamic_slice_in_dim(metric, offset, group * square, 1)
    weights = lax.dynamic_slice_in_dim(mass_weights, offset, group * square, 0)
    values = jnp.einsum("cmn,mz->czn", spread, synthesis, precision=HIGH)
    along_z = jnp.einsum("cmn,mz->czn", spread, spanwise, precision=HIGH)
    along_xi = jnp.einsum("czk,kn->czn", values, xi_matrix, precision=HIGH)
    along_eta = jnp.einsum("czk,kn->czn", values, eta_matrix, precision=HIGH)
    grad_x = factors[0] * along_xi + factors[2] * along_eta
    grad_y = factors[1] * along_xi + factors[3] * along_eta
    weighted = weights * (values[0] * grad_x + values[1] * grad_y + values[2] * along_z)
    coeffs = jnp.einsum("czn,mz->cmn", weighted, analysis, precision=HIGH)
    coeffs = lax.all_to_all(coeffs, "fourier", split_axis=1, concat_axis=2, tiled=True)
    last = NP - 1
    reach = square - last
    joined = add_shifted(coeffs, coeffs, reach, lambda n: n % NP == last)
    joined = add_shifted(joined, coeffs, -reach, lambda n: n % NP == 0)
    below, above = rim_exchange(joined, joined)
    result = add_shifted(joined, below, last * NP, lambda n: n % square < NP)
    return add_shifted(result, above, -last * NP, lambda n: n % square >= last * NP)


def shards(velocity, metric, mass_weights):
    plan = Plan(lax.axis_size("fourier"), velocity.shape[1], velocity.shape[2])
    step = chunked if plan.fits else plain
    return step(plan, velocity, metric, mass_weights)


def solution(mesh):
    in_specs = (P(None, "fourier", "elem"), P(None, "elem"), P("elem"))
    out_specs = P(None, "fourier", "elem")
    return jax.shard_map(shards, mesh=mesh, in_specs=in_specs, out_specs=out_specs, check_vma=False)
```

```python
import functools

import jax
import jax.numpy as jnp
import ml_dtypes
import numpy as np
from jax import lax
from jax.experimental import pallas as pl
from jax.experimental.pallas import tpu as pltpu
from jax.sharding import PartitionSpec as P

NP = 9
HIGH = lax.Precision.HIGHEST
BF = jnp.bfloat16
F32 = jnp.float32
LANES = 256
CHUNKS = 2
VMEM_LIMIT = 40 << 20


def gll_diff():
    half = [0.3631174638261782, 0.6771862795107377, 0.8997579954114602, 1.0]
    nodes = np.array([-v for v in half[::-1]] + [0.0] + half)
    points = nodes.shape[0]
    gaps = nodes[:, None] - nodes[None, :] + np.eye(points)
    bary = 1.0 / np.prod(gaps, axis=1)
    matrix = bary[None, :] / bary[:, None] / gaps
    matrix[np.arange(points), np.arange(points)] = 0.0
    matrix[np.arange(points), np.arange(points)] = -matrix.sum(axis=1)
    return matrix


def fourier_tables(planes):
    index = np.arange(planes)
    wave = (index + 1) // 2
    angles = 2.0 * np.pi * ((wave[:, None] * index[None, :]) % planes) / planes
    cosine_rows = ((index % 2 == 1) | (index == 0))[:, None]
    synthesis = np.where(cosine_rows, np.cos(angles), np.sin(angles))
    rate = wave * (8.0 / planes)
    rate[planes - 1] = 0.0
    spanwise = np.where(cosine_rows, -rate[:, None] * np.sin(angles), rate[:, None] * np.cos(angles))
    scale = np.where((index == 0) | (index == planes - 1), 1.0, 2.0) / planes
    analysis = synthesis * scale[:, None]
    return synthesis, spanwise, analysis


def halves(table):
    table = np.asarray(table, np.float32)
    high = table.astype(ml_dtypes.bfloat16)
    low = (table - high.astype(np.float32)).astype(ml_dtypes.bfloat16)
    return high, low


class Plan:
    def __init__(self, count, modes, nodes):
        self.count, self.modes, self.nodes = count, modes, nodes
        self.planes = count * modes
        self.elements = nodes // (NP * NP)
        self.main = modes // 16 * 16
        self.left = modes - self.main
        self.per_piece = self.elements // (count * CHUNKS)
        self.width = self.per_piece * NP * NP
        self.columns = self.per_piece * (NP - 1) + 1
        self.rows = 3 * self.main + 8
        self.pieces = CHUNKS * count
        self.joined = self.columns * NP
        self.stride = 7 * 128
        self.seam = -(-(count * self.width - self.width + NP * NP) // self.stride) * self.stride
        self.fits = (
            self.main > 0
            and 3 * self.left <= 8
            and self.elements % (count * CHUNKS) == 0
            and self.per_piece > 0
            and 128 < self.joined <= self.width <= LANES
            and self.seam <= count * self.width - NP * NP
            and self.columns <= 32
            and self.planes % 16 == 0
        )

    def lane(self, a, column):
        if column == 0:
            return a
        if column == self.columns - 1:
            return NP + a
        return 2 * NP + a * (self.columns - 2) + column - 1

    def tables(self):
        synthesis, spanwise, analysis = fourier_tables(self.planes)
        source = np.arange(self.count)
        main = (source[:, None] * self.modes + np.arange(self.main)[None, :]).reshape(-1)
        both = []
        for table in (synthesis, spanwise):
            high, low = halves(table.T[:, main])
            both.append(np.concatenate([high, high, low], axis=1))
        forward = np.stack(both)
        forward_left = np.zeros((3, 2, self.planes, 3 * 8 * self.count), ml_dtypes.bfloat16)
        back_left = np.zeros((3, 8 * self.count, 3 * self.planes), ml_dtypes.bfloat16)
        for c in range(3):
            for kind, table in enumerate((synthesis, spanwise)):
                wide = np.zeros((self.planes, 8 * self.count))
                for s in range(self.count):
                    for r in range(self.left):
                        wide[:, 8 * s + self.left * c + r] = table[s * self.modes + self.main + r]
                high, low = halves(wide)
                forward_left[c, kind] = np.concatenate([high, high, low], axis=1)
            tall = np.zeros((8 * self.count, self.planes))
            for s in range(self.count):
                for r in range(self.left):
                    tall[8 * s + self.left * c + r] = analysis[s * self.modes + self.main + r]
            high, low = halves(tall)
            back_left[c] = np.concatenate([high, high, low], axis=1)
        high, low = halves(analysis[main])
        back = np.concatenate([high, high, low], axis=1)
        return forward, forward_left, back, back_left

    def slopes(self):
        slopes = gll_diff()
        eye_elem, eye_side = np.eye(self.per_piece), np.eye(NP)
        wide = np.zeros((LANES, 2 * LANES))
        wide[: self.width, : self.width] = np.kron(eye_elem, np.kron(eye_side, slopes.T))
        wide[: self.width, LANES : LANES + self.width] = np.kron(eye_elem, np.kron(slopes.T, eye_side))
        high, low = halves(wide)
        return np.concatenate([high, high, low], axis=0)

    def assembly(self):
        join = np.zeros((3, LANES, 2 * LANES))
        rims = np.zeros((3, LANES, LANES))
        expand = np.zeros((LANES, LANES))
        for e in range(self.per_piece):
            for a in range(NP):
                for b in range(NP):
                    node, column = (e * NP + a) * NP + b, e * (NP - 1) + b
                    lane = self.lane(a, column)
                    expand[lane, node] = 1.0
                    for c in range(3):
                        join[c, node, lane] = 1.0
                        if a == 0:
                            join[c, node, LANES + 32 * c + column] = 1.0
                        if a == NP - 1:
                            join[c, node, LANES + 128 + 32 * c + column] = 1.0
        for c in range(3):
            for column in range(self.columns):
                rims[c, 32 * c + column, self.lane(0, column)] = 1.0
                rims[c, 128 + 32 * c + column, self.lane(NP - 1, column)] = 1.0
        kind = ml_dtypes.bfloat16
        join, rims, expand = join.astype(kind), rims.astype(kind), expand.astype(kind)
        return (
            np.concatenate([join, join], axis=1),
            np.concatenate([rims, rims], axis=1),
            np.concatenate([expand, expand], axis=0),
        )


def split(x):
    high = x.astype(BF)
    low = (x - high.astype(F32)).astype(BF)
    return high, low


def dot(a, b):
    return jnp.dot(a, b, preferred_element_type=F32)


def lane_ids():
    return lax.broadcasted_iota(jnp.int32, (8, 128), 1)


def put_rest(block, rest, rows, wide):
    lanes = lane_ids()
    count = -(-(rows // 8) * wide // 128)
    tiles = [None] * (count + 1)
    for t in range(rows // 8):
        tile, shift = t * wide // 128, t * wide % 128
        x = jnp.where(lanes < wide, rest[8 * t : 8 * t + 8, :], 0.0)
        if shift:
            x = pltpu.roll(x, shift, 1)
        parts = [(tile, jnp.where(lanes >= shift, x, 0.0) if shift else x)]
        if shift + wide > 128:
            parts.append((tile + 1, jnp.where(lanes < shift, x, 0.0)))
        for g, part in parts:
            tiles[g] = part if tiles[g] is None else tiles[g] + part
    for g in range(count):
        block[rows + 8 * g : rows + 8 * g + 8, :] = tiles[g]


def get_rest(block, t, rows, wide):
    lanes = lane_ids()
    tile, shift = t * wide // 128, t * wide % 128
    at = rows + 8 * tile
    x = block[at : at + 8, :]
    if shift + wide > 128:
        x = jnp.where(lanes >= shift, x, block[at + 8 : at + 16, :])
    return pltpu.roll(x, 128 - shift, 1) if shift else x


def wire_rows(rows, wide):
    return rows + 8 * (-(-(rows // 8) * wide // 128))


def by_step(steps, outs, buf):
    for s, out in enumerate(outs):
        out[...] = buf[steps[s]]


def pack_piece(plan, piece, v_ref, block, rest):
    start = piece * plan.width
    base = start // 128 * 128
    shift = start - base
    wide = LANES + 128
    tails = []
    for c in range(3):
        x = v_ref[c, : plan.main, base : base + wide]
        x = pltpu.roll(x, wide - shift, 1) if shift else x
        block[plan.main * c : plan.main * (c + 1), :] = x[:, :128]
        rest[plan.main * c : plan.main * (c + 1), :] = x[:, 128:LANES]
        if plan.left:
            tails.append(v_ref[c, plan.main : plan.modes, base : base + wide])
    tails.append(jnp.zeros((8 - 3 * plan.left, wide), F32))
    x = jnp.concatenate(tails, axis=0)
    x = pltpu.roll(x, wide - shift, 1) if shift else x
    block[3 * plan.main : plan.rows, :] = x[:, :128]
    rest[3 * plan.main : plan.rows, :] = x[:, 128:LANES]
    put_rest(block, rest, plan.rows, plan.width - 128)


def pack_first_kernel(plan, to_ref, v_hbm, *refs):
    outs, (held, buf, rest, sems) = refs[:-4], refs[-4:]
    reach = held.shape[2]
    copies = [
        pltpu.make_async_copy(v_hbm.at[c, :, pl.ds(0, reach)], held.at[c], sems.at[c]) for c in range(3)
    ]
    for copy in copies:
        copy.start()
    for copy in copies:
        copy.wait()
    for j in range(plan.count):
        pack_piece(plan, j, held, buf.at[j], rest)
    by_step(to_ref, outs, buf)


def pack_second_kernel(plan, gate_ref, v_ref, out_ref, rest):
    for j in range(plan.count):
        pack_piece(plan, plan.count + j, v_ref, out_ref.at[j], rest)


def synth_kernel(plan, joined, from_ref, *refs):
    count, main = plan.count, plan.main
    blocks, refs = (refs[:1], refs[1:]) if joined else (refs[:count], refs[count:])
    t_ref, tl_ref, d_ref, join_ref, f_ref, w_ref, low_ref, up_ref, v3, raw, l3, u, dz = refs
    deep = main * count
    wide = plan.width - 128
    for s in range(count):
        source, block = (s, blocks[0].at[s]) if joined else (from_ref[s], blocks[s])
        at = source * main
        for c in range(3):
            rest = [get_rest(block, main // 8 * c + i, plan.rows, wide) for i in range(main // 8)]
            x = jnp.concatenate([block[main * c : main * (c + 1), :], jnp.concatenate(rest, axis=0)], axis=1)
            high, low = split(x)
            for i, part in enumerate((high, low, high)):
                where = i * deep + at
                v3[c, pl.ds(where if joined else pl.multiple_of(where, 16), main), :] = part
        rest = get_rest(block, 3 * main // 8, plan.rows, wide)
        where = source * 8
        x = jnp.concatenate([block[3 * main : plan.rows, :], rest], axis=1)
        raw[pl.ds(where if joined else pl.multiple_of(where, 8), 8), :] = x
    high, low = split(raw[...])
    l3[...] = jnp.concatenate([high, low, high], axis=0)

    @pl.loop(0, 3)
    def _(c):
        u[c] = dot(t_ref[0], v3[c]) + dot(tl_ref[c, 0], l3[...])
        dz[c] = dot(t_ref[1], v3[c]) + dot(tl_ref[c, 1], l3[...])

    low_ref[...] = jnp.zeros_like(low_ref)
    up_ref[...] = jnp.zeros_like(up_ref)

    @pl.loop(0, 3)
    def _(c):
        high, low = split(u[c])
        slope = dot(jnp.concatenate([high, low, high], axis=1), d_ref[...])
        along_xi, along_eta = slope[:, :LANES], slope[:, LANES:]
        grad_x = f_ref[0:1, :] * along_xi + f_ref[2:3, :] * along_eta
        grad_y = f_ref[1:2, :] * along_xi + f_ref[3:4, :] * along_eta
        weighted = f_ref[4:5, :] * (u[0] * grad_x + u[1] * grad_y + u[2] * dz[c])
        high, low = split(weighted)
        joined = dot(jnp.concatenate([high, low], axis=1), join_ref[c])
        w_ref[c] = joined[:, :LANES]
        low_ref[...] += joined[:, LANES : LANES + 128]
        up_ref[...] += joined[:, LANES + 128 :]


def analyse_kernel(plan, joined, to_ref, w_ref, below_ref, above_ref, a_ref, al_ref, rims_ref, *refs):
    outs, (w3, tail, rest) = (refs[:1], refs[1:]) if joined else (refs[: plan.count], refs[plan.count + 1 :])
    buf = outs[0] if joined else refs[plan.count]
    count, main = plan.count, plan.main
    high, low = split(jnp.concatenate([below_ref[...], above_ref[...]], axis=1))
    rims = jnp.concatenate([high, low], axis=1)
    tail[...] = jnp.zeros_like(tail)

    @pl.loop(0, 3)
    def _(c):
        high, low = split(w_ref[c] + dot(rims, rims_ref[c]))
        w3[...] = jnp.concatenate([high, low, high], axis=0)
        coeffs = dot(a_ref[...], w3[...])
        rows = pl.ds(pl.multiple_of(c * main, main), main)
        for d in range(count):
            buf[d, rows, :] = coeffs[main * d : main * (d + 1), :128]
            rest[d, rows, :] = coeffs[main * d : main * (d + 1), 128:]
        tail[...] += dot(al_ref[c], w3[...])

    for d in range(count):
        buf[d, 3 * main : plan.rows, :] = tail[8 * d : 8 * (d + 1), :128]
        rest[d, 3 * main : plan.rows, :] = tail[8 * d : 8 * (d + 1), 128:]
        put_rest(buf.at[d], rest.at[d], plan.rows, plan.joined - 128)
    if not joined:
        by_step(to_ref, outs, buf)


def unpack_pieces(plan, pieces, held, e_ref, lhs, grown, total, base):
    rows, wide = plan.rows, plan.joined - 128
    pad = -(-rows // 16) * 16
    lanes = lax.broadcasted_iota(jnp.int32, (1, 128), 1)
    for n, i in enumerate(pieces):
        x = held[i][:rows, :]
        if i - 1 in held:
            x = x + jnp.where(lanes < NP, pltpu.roll(held[i - 1][:rows, :], 128 - NP, 1), 0.0)
        if i + 1 in held:
            inside = (lanes >= NP) & (lanes < 2 * NP)
            x = x + jnp.where(inside, pltpu.roll(held[i + 1][:rows, :], NP, 1), 0.0)
        rest = jnp.concatenate([get_rest(held[i], t, rows, wide) for t in range(rows // 8)], axis=0)
        x = jnp.concatenate([x, rest], axis=1)
        if pad > rows:
            x = jnp.concatenate([x, jnp.zeros((pad - rows, LANES), F32)], axis=0)
        high, low = split(x)
        lhs[pad * n : pad * (n + 1), :] = jnp.concatenate([high, low], axis=1)
    grown[...] = dot(lhs[...], e_ref[...])
    written = set()
    for n, i in enumerate(pieces):
        start = i * plan.width - base
        tile, shift = start // 128, start % 128
        for half in range(2):
            x = grown[pad * n : pad * n + rows, 128 * half : 128 * (half + 1)]
            x = pltpu.roll(x, shift, 1) if shift else x
            for g, keep in ((tile + half, lanes >= shift), (tile + half + 1, lanes < shift)):
                if g < 0 or 128 * g >= total.shape[1] or (g == tile + half + 1 and not shift):
                    continue
                part = jnp.where(keep, x, 0.0)
                at = slice(128 * g, 128 * (g + 1))
                total[:, at] = total[:, at] + part if g in written else part
                written.add(g)


def write_out(plan, total, out_ref, lanes):
    for c in range(3):
        out_ref[c, : plan.main, :] = total[plan.main * c : plan.main * (c + 1), lanes]
        if plan.left:
            at = 3 * plan.main + plan.left * c
            out_ref[c, plan.main :, :] = total[at : at + plan.left, lanes]


def unpack_first_kernel(plan, gate_ref, block_ref, e_ref, out_ref, lhs, grown, total):
    held = {i: block_ref.at[i] for i in range(plan.count)}
    unpack_pieces(plan, range(plan.count), held, e_ref, lhs, grown, total, 0)
    write_out(plan, total, out_ref, slice(0, out_ref.shape[2]))


def unpack_second_kernel(plan, from_ref, before_ref, old_ref, e_ref, *refs):
    blocks, (out_ref, buf, lhs, grown, total) = refs[: plan.count], refs[plan.count :]
    step = pl.program_id(0)

    @pl.when(step == 0)
    def _():
        for s in range(plan.count):
            buf[from_ref[s]] = blocks[s][...]
        held = {plan.count + j: buf.at[j] for j in range(plan.count)}
        held[plan.count - 1] = before_ref.at[0]
        unpack_pieces(plan, range(plan.count - 1, plan.pieces), held, e_ref, lhs, grown, total, plan.seam)

    for i in range(total.shape[1] // plan.stride):

        @pl.when(step == i)
        def _():
            write_out(plan, total, out_ref, slice(i * plan.stride, (i + 1) * plan.stride))


def smem():
    return pl.BlockSpec(memory_space=pltpu.SMEM)


def vmem():
    return pl.BlockSpec(memory_space=pltpu.VMEM)


def hbm():
    return pl.BlockSpec(memory_space=pl.ANY)


def params():
    return pltpu.CompilerParams(vmem_limit_bytes=VMEM_LIMIT)


def cost(flops, size):
    return pl.CostEstimate(flops=int(flops), bytes_accessed=int(size), transcendentals=0)


def pack_first(plan, to, velocity):
    last = (plan.count - 1) * plan.width
    reach = last // 128 * 128 + LANES + 128
    tall = wire_rows(plan.rows, plan.width - 128)
    return pl.pallas_call(
        functools.partial(pack_first_kernel, plan),
        in_specs=[smem(), hbm()],
        out_specs=[vmem()] * plan.count,
        out_shape=[jax.ShapeDtypeStruct((tall, 128), F32)] * plan.count,
        scratch_shapes=[
            pltpu.VMEM((3, plan.modes, reach), F32),
            pltpu.VMEM((plan.count, tall, 128), F32),
            pltpu.VMEM((plan.rows, 128), F32),
            pltpu.SemaphoreType.DMA((3,)),
        ],
        compiler_params=params(),
        cost_estimate=cost(0, 8 * plan.count * tall * 128),
        name="pack_first",
    )(to, velocity)


def pack_second(plan, gate, velocity):
    span = -(-plan.nodes // 128) * 128
    tall = wire_rows(plan.rows, plan.width - 128)
    return pl.pallas_call(
        functools.partial(pack_second_kernel, plan),
        grid=(1,),
        in_specs=[smem(), pl.BlockSpec((3, plan.modes, span), lambda i: (0, 0, 0))],
        out_specs=pl.BlockSpec((plan.count, tall, 128), lambda i: (0, 0, 0)),
        out_shape=jax.ShapeDtypeStruct((plan.count, tall, 128), F32),
        scratch_shapes=[pltpu.VMEM((plan.rows, 128), F32)],
        compiler_params=params(),
        cost_estimate=cost(0, 8 * plan.count * tall * 128),
        name="pack_second",
    )(gate, velocity)


def synth(plan, name, came, blocks, tables, factors):
    joined = not isinstance(blocks, list)
    blocks = [blocks] if joined else blocks
    deep = plan.main * plan.count
    small = 8 * plan.count
    field = jax.ShapeDtypeStruct((3, plan.planes, LANES), F32)
    rim = jax.ShapeDtypeStruct((plan.planes, 128), F32)
    return pl.pallas_call(
        functools.partial(synth_kernel, plan, joined),
        in_specs=[smem()] + [vmem()] * (len(blocks) + 5),
        out_specs=[vmem()] * 3,
        out_shape=[field, rim, rim],
        scratch_shapes=[
            pltpu.VMEM((3, 3 * deep, LANES), BF),
            pltpu.VMEM((small, LANES), F32),
            pltpu.VMEM((3 * small, LANES), BF),
            pltpu.VMEM((3, plan.planes, LANES), F32),
            pltpu.VMEM((3, plan.planes, LANES), F32),
        ],
        compiler_params=params(),
        cost_estimate=cost(3 * 2 * plan.planes * LANES * (6 * deep + 6 * LANES + 4 * LANES), 12 << 20),
        name=name,
    )(came, *blocks, *tables, factors)


def analyse(plan, name, joined, to, field, below, above, tables):
    count = plan.count
    tall = wire_rows(plan.rows, plan.joined - 128)
    if joined:
        shape, specs, extra = jax.ShapeDtypeStruct((count, tall, 128), F32), vmem(), []
    else:
        shape, specs = [jax.ShapeDtypeStruct((tall, 128), F32)] * count, [vmem()] * count
        extra = [pltpu.VMEM((count, tall, 128), F32)]
    return pl.pallas_call(
        functools.partial(analyse_kernel, plan, joined),
        in_specs=[smem()] + [vmem()] * 6,
        out_specs=specs,
        out_shape=shape,
        scratch_shapes=extra
        + [
            pltpu.VMEM((3 * plan.planes, LANES), BF),
            pltpu.VMEM((8 * count, LANES), F32),
            pltpu.VMEM((count, plan.rows, 128), F32),
        ],
        compiler_params=params(),
        cost_estimate=cost(3 * 2 * plan.planes * LANES * 3 * plan.planes, 6 << 20),
        name=name,
    )(to, field, below, above, *tables)


def unpack_scratch(plan, pieces, span):
    pad = -(-plan.rows // 16) * 16
    return [
        pltpu.VMEM((pieces * pad, 2 * LANES), BF),
        pltpu.VMEM((pieces * pad, LANES), F32),
        pltpu.VMEM((plan.rows, span), F32),
    ]


def unpack_first(plan, gate, blocks, expand):
    out = jax.ShapeDtypeStruct((3, plan.modes, plan.nodes), F32)
    return pl.pallas_call(
        functools.partial(unpack_first_kernel, plan),
        grid=(1,),
        in_specs=[smem(), vmem(), vmem()],
        out_specs=pl.BlockSpec((3, plan.modes, plan.seam), lambda i: (0, 0, 0)),
        out_shape=out,
        scratch_shapes=unpack_scratch(plan, plan.count, plan.seam),
        compiler_params=params(),
        cost_estimate=cost(2 * plan.count * plan.rows * LANES * 2 * LANES, 4 << 20),
        name="unpack_first",
    )(gate, blocks, expand)


def unpack_second(plan, came, before, old, blocks, expand):
    tall = blocks[0].shape[0]
    steps = -(-(plan.nodes - plan.seam) // plan.stride)
    skip = plan.seam // plan.stride
    return pl.pallas_call(
        functools.partial(unpack_second_kernel, plan),
        grid=(steps,),
        in_specs=[
            smem(),
            pl.BlockSpec((1, tall, 128), lambda i: (plan.count - 1, 0, 0)),
            hbm(),
            pl.BlockSpec(expand.shape, lambda i: (0, 0)),
        ]
        + [pl.BlockSpec((tall, 128), lambda i: (0, 0))] * plan.count,
        out_specs=pl.BlockSpec((3, plan.modes, plan.stride), lambda i: (0, 0, i + skip)),
        out_shape=jax.ShapeDtypeStruct((3, plan.modes, plan.nodes), F32),
        scratch_shapes=[pltpu.VMEM((plan.count, tall, 128), F32)]
        + unpack_scratch(plan, plan.count + 1, steps * plan.stride),
        input_output_aliases={2: 0},
        compiler_params=params(),
        cost_estimate=cost(2 * plan.count * plan.rows * LANES * 2 * LANES, 4 << 20),
        name="unpack_second",
    )(came, before, old, expand, *blocks)


def permutes(blocks, count):
    outs = [blocks[0]]
    for s in range(1, count):
        outs.append(lax.ppermute(blocks[s], "fourier", [(k, (k + s) % count) for k in range(count)]))
    return outs


def all_at_once(blocks):
    return lax.all_to_all(blocks, "fourier", split_axis=0, concat_axis=0, tiled=True)


def rim_exchange(low, up):
    ends = lax.axis_size("elem") - 1
    below = lax.ppermute(up, "elem", [(i, i + 1) for i in range(ends)])
    above = lax.ppermute(low, "elem", [(i + 1, i) for i in range(ends)])
    return below, above


def after(x, other):
    return lax.optimization_barrier((x, other))[0]


def chunked(plan, velocity, metric, mass_weights):
    count = plan.count
    here = lax.axis_index("fourier").astype(jnp.int32)
    steps = jnp.arange(count, dtype=jnp.int32)
    to, came = (here + steps) % count, (here - steps + count) % count
    forward, forward_left, back, back_left = (jnp.asarray(t) for t in plan.tables())
    slopes = jnp.asarray(plan.slopes())
    join, rims, expand = (jnp.asarray(t) for t in plan.assembly())
    local = jnp.concatenate([metric, mass_weights[None], jnp.zeros((3, plan.nodes), F32)], axis=0)
    tables = (forward, forward_left, slopes, join)
    back_tables = (back, back_left, rims)
    factors = []
    for q in range(CHUNKS):
        start = (here + q * count) * plan.width
        cut = lax.dynamic_slice_in_dim(local, start, plan.width, 1)
        factors.append(jnp.pad(cut, ((0, 0), (0, LANES - plan.width))))

    sent = pack_first(plan, to, velocity)
    spread = permutes(sent, count)
    second = pack_second(plan, after(to, sent[1]), velocity)
    second = all_at_once(after(second, spread))
    field, low, up = synth(plan, "synth_first", came, spread, tables, factors[0])
    below, above = rim_exchange(low, up)
    back_first = analyse(plan, "analyse_first", True, to, field, below, above, back_tables)
    back_first = all_at_once(after(back_first, second))
    field, low, up = synth(plan, "synth_second", came, second, tables, factors[1])
    below, above = rim_exchange(low, up)
    back_second = analyse(plan, "analyse_second", False, to, field, below, above, back_tables)
    returned = permutes(after(back_second, back_first), count)
    half = unpack_first(plan, to, back_first, expand)
    return unpack_second(plan, came, back_first, half, returned, expand)


def add_shifted(field, source, reach, side):
    count = field.shape[-1]
    node = np.arange(count)
    keep = side(node) & (node + reach >= 0) & (node + reach < count)
    pads = [(0, 0)] * (field.ndim - 1)
    if reach > 0:
        moved = jnp.pad(source[..., reach:], pads + [(0, reach)])
    else:
        moved = jnp.pad(source[..., :reach], pads + [(-reach, 0)])
    return field + jnp.where(jnp.asarray(keep), moved, 0.0)


def plain(plan, velocity, metric, mass_weights):
    count, square = plan.count, NP * NP
    synthesis, spanwise, analysis = (jnp.asarray(t, F32) for t in fourier_tables(plan.planes))
    slopes = gll_diff()
    group = plan.elements // count
    eye_elem, eye_side = np.eye(group), np.eye(NP)
    xi_matrix = jnp.asarray(np.kron(eye_elem, np.kron(eye_side, slopes.T)), F32)
    eta_matrix = jnp.asarray(np.kron(eye_elem, np.kron(slopes.T, eye_side)), F32)
    spread = lax.all_to_all(velocity, "fourier", split_axis=2, concat_axis=1, tiled=True)
    offset = lax.axis_index("fourier") * group * square
    factors = lax.dynamic_slice_in_dim(metric, offset, group * square, 1)
    weights = lax.dynamic_slice_in_dim(mass_weights, offset, group * square, 0)
    values = jnp.einsum("cmn,mz->czn", spread, synthesis, precision=HIGH)
    along_z = jnp.einsum("cmn,mz->czn", spread, spanwise, precision=HIGH)
    along_xi = jnp.einsum("czk,kn->czn", values, xi_matrix, precision=HIGH)
    along_eta = jnp.einsum("czk,kn->czn", values, eta_matrix, precision=HIGH)
    grad_x = factors[0] * along_xi + factors[2] * along_eta
    grad_y = factors[1] * along_xi + factors[3] * along_eta
    weighted = weights * (values[0] * grad_x + values[1] * grad_y + values[2] * along_z)
    coeffs = jnp.einsum("czn,mz->cmn", weighted, analysis, precision=HIGH)
    coeffs = lax.all_to_all(coeffs, "fourier", split_axis=1, concat_axis=2, tiled=True)
    last = NP - 1
    reach = square - last
    joined = add_shifted(coeffs, coeffs, reach, lambda n: n % NP == last)
    joined = add_shifted(joined, coeffs, -reach, lambda n: n % NP == 0)
    below, above = rim_exchange(joined, joined)
    result = add_shifted(joined, below, last * NP, lambda n: n % square < NP)
    return add_shifted(result, above, -last * NP, lambda n: n % square >= last * NP)


def shards(velocity, metric, mass_weights):
    plan = Plan(lax.axis_size("fourier"), velocity.shape[1], velocity.shape[2])
    step = chunked if plan.fits else plain
    return step(plan, velocity, metric, mass_weights)


def solution(mesh):
    in_specs = (P(None, "fourier", "elem"), P(None, "elem"), P("elem"))
    out_specs = P(None, "fourier", "elem")
    return jax.shard_map(shards, mesh=mesh, in_specs=in_specs, out_specs=out_specs, check_vma=False)
```

```python
import functools

import jax
import jax.numpy as jnp
import ml_dtypes
import numpy as np
from jax import lax
from jax.experimental import pallas as pl
from jax.experimental.pallas import tpu as pltpu
from jax.sharding import PartitionSpec as P

NP = 9
HIGH = lax.Precision.HIGHEST
BF = jnp.bfloat16
F32 = jnp.float32
LANES = 256
CHUNKS = 2
VMEM_LIMIT = 40 << 20


def gll_diff():
    half = [0.3631174638261782, 0.6771862795107377, 0.8997579954114602, 1.0]
    nodes = np.array([-v for v in half[::-1]] + [0.0] + half)
    points = nodes.shape[0]
    gaps = nodes[:, None] - nodes[None, :] + np.eye(points)
    bary = 1.0 / np.prod(gaps, axis=1)
    matrix = bary[None, :] / bary[:, None] / gaps
    matrix[np.arange(points), np.arange(points)] = 0.0
    matrix[np.arange(points), np.arange(points)] = -matrix.sum(axis=1)
    return matrix


def fourier_tables(planes):
    index = np.arange(planes)
    wave = (index + 1) // 2
    angles = 2.0 * np.pi * ((wave[:, None] * index[None, :]) % planes) / planes
    cosine_rows = ((index % 2 == 1) | (index == 0))[:, None]
    synthesis = np.where(cosine_rows, np.cos(angles), np.sin(angles))
    rate = wave * (8.0 / planes)
    rate[planes - 1] = 0.0
    spanwise = np.where(cosine_rows, -rate[:, None] * np.sin(angles), rate[:, None] * np.cos(angles))
    scale = np.where((index == 0) | (index == planes - 1), 1.0, 2.0) / planes
    analysis = synthesis * scale[:, None]
    return synthesis, spanwise, analysis


def halves(table):
    table = np.asarray(table, np.float32)
    high = table.astype(ml_dtypes.bfloat16)
    low = (table - high.astype(np.float32)).astype(ml_dtypes.bfloat16)
    return high, low


class Plan:
    def __init__(self, count, modes, nodes):
        self.count, self.modes, self.nodes = count, modes, nodes
        self.planes = count * modes
        self.elements = nodes // (NP * NP)
        self.main = modes // 16 * 16
        self.left = modes - self.main
        self.per_piece = self.elements // (count * CHUNKS)
        self.width = self.per_piece * NP * NP
        self.columns = self.per_piece * (NP - 1) + 1
        self.rows = 3 * self.main + 8
        self.pieces = CHUNKS * count
        self.joined = self.columns * NP
        self.stride = 7 * 128
        self.seam = -(-(count * self.width - self.width + NP * NP) // self.stride) * self.stride
        self.fits = (
            self.main > 0
            and 3 * self.left <= 8
            and self.elements % (count * CHUNKS) == 0
            and self.per_piece > 0
            and 128 < self.joined <= self.width <= LANES
            and self.seam <= count * self.width - NP * NP
            and self.columns <= 32
            and self.planes % 16 == 0
        )

    def lane(self, a, column):
        if column == 0:
            return a
        if column == self.columns - 1:
            return NP + a
        return 2 * NP + a * (self.columns - 2) + column - 1

    def tables(self):
        synthesis, spanwise, analysis = fourier_tables(self.planes)
        source = np.arange(self.count)
        main = (source[:, None] * self.modes + np.arange(self.main)[None, :]).reshape(-1)
        both = []
        for table in (synthesis, spanwise):
            high, low = halves(table.T[:, main])
            both.append(np.concatenate([high, high, low], axis=1))
        forward = np.stack(both)
        forward_left = np.zeros((3, 2, self.planes, 3 * 8 * self.count), ml_dtypes.bfloat16)
        back_left = np.zeros((3, 8 * self.count, 3 * self.planes), ml_dtypes.bfloat16)
        for c in range(3):
            for kind, table in enumerate((synthesis, spanwise)):
                wide = np.zeros((self.planes, 8 * self.count))
                for s in range(self.count):
                    for r in range(self.left):
                        wide[:, 8 * s + self.left * c + r] = table[s * self.modes + self.main + r]
                high, low = halves(wide)
                forward_left[c, kind] = np.concatenate([high, high, low], axis=1)
            tall = np.zeros((8 * self.count, self.planes))
            for s in range(self.count):
                for r in range(self.left):
                    tall[8 * s + self.left * c + r] = analysis[s * self.modes + self.main + r]
            high, low = halves(tall)
            back_left[c] = np.concatenate([high, high, low], axis=1)
        high, low = halves(analysis[main])
        back = np.concatenate([high, high, low], axis=1)
        return forward, forward_left, back, back_left

    def slopes(self):
        slopes = gll_diff()
        eye_elem, eye_side = np.eye(self.per_piece), np.eye(NP)
        wide = np.zeros((LANES, 2 * LANES))
        wide[: self.width, : self.width] = np.kron(eye_elem, np.kron(eye_side, slopes.T))
        wide[: self.width, LANES : LANES + self.width] = np.kron(eye_elem, np.kron(slopes.T, eye_side))
        high, low = halves(wide)
        return np.concatenate([high, high, low], axis=0)

    def assembly(self):
        join = np.zeros((3, LANES, 2 * LANES))
        rims = np.zeros((3, LANES, LANES))
        expand = np.zeros((LANES, LANES))
        for e in range(self.per_piece):
            for a in range(NP):
                for b in range(NP):
                    node, column = (e * NP + a) * NP + b, e * (NP - 1) + b
                    lane = self.lane(a, column)
                    expand[lane, node] = 1.0
                    for c in range(3):
                        join[c, node, lane] = 1.0
                        if a == 0:
                            join[c, node, LANES + 32 * c + column] = 1.0
                        if a == NP - 1:
                            join[c, node, LANES + 128 + 32 * c + column] = 1.0
        for c in range(3):
            for column in range(self.columns):
                rims[c, 32 * c + column, self.lane(0, column)] = 1.0
                rims[c, 128 + 32 * c + column, self.lane(NP - 1, column)] = 1.0
        kind = ml_dtypes.bfloat16
        join, rims, expand = join.astype(kind), rims.astype(kind), expand.astype(kind)
        return (
            np.concatenate([join, join], axis=1),
            np.concatenate([rims, rims], axis=1),
            np.concatenate([expand, expand], axis=0),
        )


def split(x):
    high = x.astype(BF)
    low = (x - high.astype(F32)).astype(BF)
    return high, low


def dot(a, b):
    return jnp.dot(a, b, preferred_element_type=F32)


def lane_ids():
    return lax.broadcasted_iota(jnp.int32, (8, 128), 1)


def put_rest(block, rest, rows, wide):
    lanes = lane_ids()
    count = -(-(rows // 8) * wide // 128)
    tiles = [None] * (count + 1)
    for t in range(rows // 8):
        tile, shift = t * wide // 128, t * wide % 128
        x = jnp.where(lanes < wide, rest[8 * t : 8 * t + 8, :], 0.0)
        if shift:
            x = pltpu.roll(x, shift, 1)
        parts = [(tile, jnp.where(lanes >= shift, x, 0.0) if shift else x)]
        if shift + wide > 128:
            parts.append((tile + 1, jnp.where(lanes < shift, x, 0.0)))
        for g, part in parts:
            tiles[g] = part if tiles[g] is None else tiles[g] + part
    for g in range(count):
        block[rows + 8 * g : rows + 8 * g + 8, :] = tiles[g]


def get_rest(block, t, rows, wide):
    lanes = lane_ids()
    tile, shift = t * wide // 128, t * wide % 128
    at = rows + 8 * tile
    x = block[at : at + 8, :]
    if shift + wide > 128:
        x = jnp.where(lanes >= shift, x, block[at + 8 : at + 16, :])
    return pltpu.roll(x, 128 - shift, 1) if shift else x


def wire_rows(rows, wide):
    return rows + 8 * (-(-(rows // 8) * wide // 128))


def by_step(steps, outs, buf):
    for s, out in enumerate(outs):
        out[...] = buf[steps[s]]


def pack_piece(plan, piece, v_ref, block, rest):
    start = piece * plan.width
    base = start // 128 * 128
    shift = start - base
    wide = LANES + 128
    tails = []
    for c in range(3):
        x = v_ref[c, : plan.main, base : base + wide]
        x = pltpu.roll(x, wide - shift, 1) if shift else x
        block[plan.main * c : plan.main * (c + 1), :] = x[:, :128]
        rest[plan.main * c : plan.main * (c + 1), :] = x[:, 128:LANES]
        if plan.left:
            tails.append(v_ref[c, plan.main : plan.modes, base : base + wide])
    tails.append(jnp.zeros((8 - 3 * plan.left, wide), F32))
    x = jnp.concatenate(tails, axis=0)
    x = pltpu.roll(x, wide - shift, 1) if shift else x
    block[3 * plan.main : plan.rows, :] = x[:, :128]
    rest[3 * plan.main : plan.rows, :] = x[:, 128:LANES]
    put_rest(block, rest, plan.rows, plan.width - 128)


def pack_first_kernel(plan, to_ref, v_hbm, *refs):
    outs, (held, buf, rest, sems) = refs[:-4], refs[-4:]
    reach = held.shape[2]
    copies = [
        pltpu.make_async_copy(v_hbm.at[c, :, pl.ds(0, reach)], held.at[c], sems.at[c]) for c in range(3)
    ]
    for copy in copies:
        copy.start()
    for copy in copies:
        copy.wait()
    for j in range(plan.count):
        pack_piece(plan, j, held, buf.at[j], rest)
    by_step(to_ref, outs, buf)


def pack_second_kernel(plan, gate_ref, v_ref, out_ref, rest):
    for j in range(plan.count):
        pack_piece(plan, plan.count + j, v_ref, out_ref.at[j], rest)


def synth_kernel(plan, joined, from_ref, *refs):
    count, main = plan.count, plan.main
    blocks, refs = (refs[:1], refs[1:]) if joined else (refs[:count], refs[count:])
    t_ref, tl_ref, d_ref, join_ref, f_ref, w_ref, low_ref, up_ref, v3, raw, l3, u, dz = refs
    deep = main * count
    wide = plan.width - 128
    for s in range(count):
        source, block = (s, blocks[0].at[s]) if joined else (from_ref[s], blocks[s])
        at = source * main
        for c in range(3):
            rest = [get_rest(block, main // 8 * c + i, plan.rows, wide) for i in range(main // 8)]
            x = jnp.concatenate([block[main * c : main * (c + 1), :], jnp.concatenate(rest, axis=0)], axis=1)
            high, low = split(x)
            for i, part in enumerate((high, low, high)):
                where = i * deep + at
                v3[c, pl.ds(where if joined else pl.multiple_of(where, 16), main), :] = part
        rest = get_rest(block, 3 * main // 8, plan.rows, wide)
        where = source * 8
        x = jnp.concatenate([block[3 * main : plan.rows, :], rest], axis=1)
        raw[pl.ds(where if joined else pl.multiple_of(where, 8), 8), :] = x
    high, low = split(raw[...])
    l3[...] = jnp.concatenate([high, low, high], axis=0)

    @pl.loop(0, 3)
    def _(c):
        u[c] = dot(t_ref[0], v3[c]) + dot(tl_ref[c, 0], l3[...])
        dz[c] = dot(t_ref[1], v3[c]) + dot(tl_ref[c, 1], l3[...])

    low_ref[...] = jnp.zeros_like(low_ref)
    up_ref[...] = jnp.zeros_like(up_ref)

    @pl.loop(0, 3)
    def _(c):
        high, low = split(u[c])
        slope = dot(jnp.concatenate([high, low, high], axis=1), d_ref[...])
        along_xi, along_eta = slope[:, :LANES], slope[:, LANES:]
        grad_x = f_ref[0:1, :] * along_xi + f_ref[2:3, :] * along_eta
        grad_y = f_ref[1:2, :] * along_xi + f_ref[3:4, :] * along_eta
        weighted = f_ref[4:5, :] * (u[0] * grad_x + u[1] * grad_y + u[2] * dz[c])
        high, low = split(weighted)
        joined = dot(jnp.concatenate([high, low], axis=1), join_ref[c])
        w_ref[c] = joined[:, :LANES]
        low_ref[...] += joined[:, LANES : LANES + 128]
        up_ref[...] += joined[:, LANES + 128 :]


def analyse_kernel(plan, joined, to_ref, w_ref, below_ref, above_ref, a_ref, al_ref, rims_ref, *refs):
    outs, (w3, tail, rest) = (refs[:1], refs[1:]) if joined else (refs[: plan.count], refs[plan.count + 1 :])
    buf = outs[0] if joined else refs[plan.count]
    count, main = plan.count, plan.main
    high, low = split(jnp.concatenate([below_ref[...], above_ref[...]], axis=1))
    rims = jnp.concatenate([high, low], axis=1)
    tail[...] = jnp.zeros_like(tail)

    @pl.loop(0, 3)
    def _(c):
        high, low = split(w_ref[c] + dot(rims, rims_ref[c]))
        w3[...] = jnp.concatenate([high, low, high], axis=0)
        coeffs = dot(a_ref[...], w3[...])
        rows = pl.ds(pl.multiple_of(c * main, main), main)
        for d in range(count):
            buf[d, rows, :] = coeffs[main * d : main * (d + 1), :128]
            rest[d, rows, :] = coeffs[main * d : main * (d + 1), 128:]
        tail[...] += dot(al_ref[c], w3[...])

    for d in range(count):
        buf[d, 3 * main : plan.rows, :] = tail[8 * d : 8 * (d + 1), :128]
        rest[d, 3 * main : plan.rows, :] = tail[8 * d : 8 * (d + 1), 128:]
        put_rest(buf.at[d], rest.at[d], plan.rows, plan.joined - 128)
    if not joined:
        by_step(to_ref, outs, buf)


def unpack_pieces(plan, pieces, held, e_ref, lhs, grown, total, base):
    rows, wide = plan.rows, plan.joined - 128
    pad = -(-rows // 16) * 16
    lanes = lax.broadcasted_iota(jnp.int32, (1, 128), 1)
    for n, i in enumerate(pieces):
        x = held[i][:rows, :]
        if i - 1 in held:
            x = x + jnp.where(lanes < NP, pltpu.roll(held[i - 1][:rows, :], 128 - NP, 1), 0.0)
        if i + 1 in held:
            inside = (lanes >= NP) & (lanes < 2 * NP)
            x = x + jnp.where(inside, pltpu.roll(held[i + 1][:rows, :], NP, 1), 0.0)
        rest = jnp.concatenate([get_rest(held[i], t, rows, wide) for t in range(rows // 8)], axis=0)
        x = jnp.concatenate([x, rest], axis=1)
        if pad > rows:
            x = jnp.concatenate([x, jnp.zeros((pad - rows, LANES), F32)], axis=0)
        high, low = split(x)
        lhs[pad * n : pad * (n + 1), :] = jnp.concatenate([high, low], axis=1)
    grown[...] = dot(lhs[...], e_ref[...])
    written = set()
    for n, i in enumerate(pieces):
        start = i * plan.width - base
        tile, shift = start // 128, start % 128
        for half in range(2):
            x = grown[pad * n : pad * n + rows, 128 * half : 128 * (half + 1)]
            x = pltpu.roll(x, shift, 1) if shift else x
            for g, keep in ((tile + half, lanes >= shift), (tile + half + 1, lanes < shift)):
                if g < 0 or 128 * g >= total.shape[1] or (g == tile + half + 1 and not shift):
                    continue
                part = jnp.where(keep, x, 0.0)
                at = slice(128 * g, 128 * (g + 1))
                total[:, at] = total[:, at] + part if g in written else part
                written.add(g)


def write_out(plan, total, out_ref, lanes):
    for c in range(3):
        out_ref[c, : plan.main, :] = total[plan.main * c : plan.main * (c + 1), lanes]
        if plan.left:
            at = 3 * plan.main + plan.left * c
            out_ref[c, plan.main :, :] = total[at : at + plan.left, lanes]


def unpack_first_kernel(plan, gate_ref, block_ref, e_ref, out_ref, lhs, grown, total):
    held = {i: block_ref.at[i] for i in range(plan.count)}
    unpack_pieces(plan, range(plan.count), held, e_ref, lhs, grown, total, 0)
    write_out(plan, total, out_ref, slice(0, out_ref.shape[2]))


def unpack_second_kernel(plan, from_ref, before_ref, old_ref, e_ref, *refs):
    blocks, (out_ref, buf, lhs, grown, total) = refs[: plan.count], refs[plan.count :]
    step = pl.program_id(0)

    @pl.when(step == 0)
    def _():
        for s in range(plan.count):
            buf[from_ref[s]] = blocks[s][...]
        held = {plan.count + j: buf.at[j] for j in range(plan.count)}
        held[plan.count - 1] = before_ref.at[0]
        unpack_pieces(plan, range(plan.count - 1, plan.pieces), held, e_ref, lhs, grown, total, plan.seam)

    for i in range(total.shape[1] // plan.stride):

        @pl.when(step == i)
        def _():
            write_out(plan, total, out_ref, slice(i * plan.stride, (i + 1) * plan.stride))


def smem():
    return pl.BlockSpec(memory_space=pltpu.SMEM)


def vmem():
    return pl.BlockSpec(memory_space=pltpu.VMEM)


def hbm():
    return pl.BlockSpec(memory_space=pl.ANY)


def params():
    return pltpu.CompilerParams(vmem_limit_bytes=VMEM_LIMIT)


def cost(flops, size):
    return pl.CostEstimate(flops=int(flops), bytes_accessed=int(size), transcendentals=0)


def pack_first(plan, to, velocity):
    last = (plan.count - 1) * plan.width
    reach = last // 128 * 128 + LANES + 128
    tall = wire_rows(plan.rows, plan.width - 128)
    return pl.pallas_call(
        functools.partial(pack_first_kernel, plan),
        in_specs=[smem(), hbm()],
        out_specs=[vmem()] * plan.count,
        out_shape=[jax.ShapeDtypeStruct((tall, 128), F32)] * plan.count,
        scratch_shapes=[
            pltpu.VMEM((3, plan.modes, reach), F32),
            pltpu.VMEM((plan.count, tall, 128), F32),
            pltpu.VMEM((plan.rows, 128), F32),
            pltpu.SemaphoreType.DMA((3,)),
        ],
        compiler_params=params(),
        cost_estimate=cost(0, 8 * plan.count * tall * 128),
        name="pack_first",
    )(to, velocity)


def pack_second(plan, gate, velocity):
    span = -(-plan.nodes // 128) * 128
    tall = wire_rows(plan.rows, plan.width - 128)
    return pl.pallas_call(
        functools.partial(pack_second_kernel, plan),
        grid=(1,),
        in_specs=[smem(), pl.BlockSpec((3, plan.modes, span), lambda i: (0, 0, 0))],
        out_specs=pl.BlockSpec((plan.count, tall, 128), lambda i: (0, 0, 0)),
        out_shape=jax.ShapeDtypeStruct((plan.count, tall, 128), F32),
        scratch_shapes=[pltpu.VMEM((plan.rows, 128), F32)],
        compiler_params=params(),
        cost_estimate=cost(0, 8 * plan.count * tall * 128),
        name="pack_second",
    )(gate, velocity)


def synth(plan, name, came, blocks, tables, factors):
    joined = not isinstance(blocks, list)
    blocks = [blocks] if joined else blocks
    deep = plan.main * plan.count
    small = 8 * plan.count
    field = jax.ShapeDtypeStruct((3, plan.planes, LANES), F32)
    rim = jax.ShapeDtypeStruct((plan.planes, 128), F32)
    return pl.pallas_call(
        functools.partial(synth_kernel, plan, joined),
        in_specs=[smem()] + [vmem()] * (len(blocks) + 5),
        out_specs=[vmem()] * 3,
        out_shape=[field, rim, rim],
        scratch_shapes=[
            pltpu.VMEM((3, 3 * deep, LANES), BF),
            pltpu.VMEM((small, LANES), F32),
            pltpu.VMEM((3 * small, LANES), BF),
            pltpu.VMEM((3, plan.planes, LANES), F32),
            pltpu.VMEM((3, plan.planes, LANES), F32),
        ],
        compiler_params=params(),
        cost_estimate=cost(3 * 2 * plan.planes * LANES * (6 * deep + 6 * LANES + 4 * LANES), 12 << 20),
        name=name,
    )(came, *blocks, *tables, factors)


def analyse(plan, name, joined, to, field, below, above, tables):
    count = plan.count
    tall = wire_rows(plan.rows, plan.joined - 128)
    if joined:
        shape, specs, extra = jax.ShapeDtypeStruct((count, tall, 128), F32), vmem(), []
    else:
        shape, specs = [jax.ShapeDtypeStruct((tall, 128), F32)] * count, [vmem()] * count
        extra = [pltpu.VMEM((count, tall, 128), F32)]
    return pl.pallas_call(
        functools.partial(analyse_kernel, plan, joined),
        in_specs=[smem()] + [vmem()] * 6,
        out_specs=specs,
        out_shape=shape,
        scratch_shapes=extra
        + [
            pltpu.VMEM((3 * plan.planes, LANES), BF),
            pltpu.VMEM((8 * count, LANES), F32),
            pltpu.VMEM((count, plan.rows, 128), F32),
        ],
        compiler_params=params(),
        cost_estimate=cost(3 * 2 * plan.planes * LANES * 3 * plan.planes, 6 << 20),
        name=name,
    )(to, field, below, above, *tables)


def unpack_scratch(plan, pieces, span):
    pad = -(-plan.rows // 16) * 16
    return [
        pltpu.VMEM((pieces * pad, 2 * LANES), BF),
        pltpu.VMEM((pieces * pad, LANES), F32),
        pltpu.VMEM((plan.rows, span), F32),
    ]


def unpack_first(plan, gate, blocks, expand):
    out = jax.ShapeDtypeStruct((3, plan.modes, plan.nodes), F32)
    return pl.pallas_call(
        functools.partial(unpack_first_kernel, plan),
        grid=(1,),
        in_specs=[smem(), vmem(), vmem()],
        out_specs=pl.BlockSpec((3, plan.modes, plan.seam), lambda i: (0, 0, 0)),
        out_shape=out,
        scratch_shapes=unpack_scratch(plan, plan.count, plan.seam),
        compiler_params=params(),
        cost_estimate=cost(2 * plan.count * plan.rows * LANES * 2 * LANES, 4 << 20),
        name="unpack_first",
    )(gate, blocks, expand)


def unpack_second(plan, came, before, old, blocks, expand):
    tall = blocks[0].shape[0]
    steps = -(-(plan.nodes - plan.seam) // plan.stride)
    skip = plan.seam // plan.stride
    return pl.pallas_call(
        functools.partial(unpack_second_kernel, plan),
        grid=(steps,),
        in_specs=[
            smem(),
            pl.BlockSpec((1, tall, 128), lambda i: (plan.count - 1, 0, 0)),
            hbm(),
            pl.BlockSpec(expand.shape, lambda i: (0, 0)),
        ]
        + [pl.BlockSpec((tall, 128), lambda i: (0, 0))] * plan.count,
        out_specs=pl.BlockSpec((3, plan.modes, plan.stride), lambda i: (0, 0, i + skip)),
        out_shape=jax.ShapeDtypeStruct((3, plan.modes, plan.nodes), F32),
        scratch_shapes=[pltpu.VMEM((plan.count, tall, 128), F32)]
        + unpack_scratch(plan, plan.count + 1, steps * plan.stride),
        input_output_aliases={2: 0},
        compiler_params=params(),
        cost_estimate=cost(2 * plan.count * plan.rows * LANES * 2 * LANES, 4 << 20),
        name="unpack_second",
    )(came, before, old, expand, *blocks)


def permutes(blocks, count):
    outs = [blocks[0]]
    for s in range(1, count):
        outs.append(lax.ppermute(blocks[s], "fourier", [(k, (k + s) % count) for k in range(count)]))
    return outs


def all_at_once(blocks):
    return lax.all_to_all(blocks, "fourier", split_axis=0, concat_axis=0, tiled=True)


def rim_exchange(low, up):
    ends = lax.axis_size("elem") - 1
    below = lax.ppermute(up, "elem", [(i, i + 1) for i in range(ends)])
    above = lax.ppermute(low, "elem", [(i + 1, i) for i in range(ends)])
    return below, above


def after(x, other):
    return lax.optimization_barrier((x, other))[0]


def chunked(plan, velocity, metric, mass_weights):
    count = plan.count
    here = lax.axis_index("fourier").astype(jnp.int32)
    steps = jnp.arange(count, dtype=jnp.int32)
    to, came = (here + steps) % count, (here - steps + count) % count
    forward, forward_left, back, back_left = (jnp.asarray(t) for t in plan.tables())
    slopes = jnp.asarray(plan.slopes())
    join, rims, expand = (jnp.asarray(t) for t in plan.assembly())
    local = jnp.concatenate([metric, mass_weights[None], jnp.zeros((3, plan.nodes), F32)], axis=0)
    tables = (forward, forward_left, slopes, join)
    back_tables = (back, back_left, rims)
    factors = []
    for q in range(CHUNKS):
        start = (here + q * count) * plan.width
        cut = lax.dynamic_slice_in_dim(local, start, plan.width, 1)
        factors.append(jnp.pad(cut, ((0, 0), (0, LANES - plan.width))))

    sent = pack_first(plan, to, velocity)
    spread = permutes(sent, count)
    second = pack_second(plan, after(to, sent[1]), velocity)
    second = all_at_once(after(second, spread))
    field, low, up = synth(plan, "synth_first", came, spread, tables, factors[0])
    below, above = rim_exchange(low, up)
    back_first = analyse(plan, "analyse_first", True, to, field, below, above, back_tables)
    back_first = all_at_once(after(back_first, second))
    field, low, up = synth(plan, "synth_second", came, second, tables, factors[1])
    below, above = rim_exchange(low, up)
    back_second = analyse(plan, "analyse_second", False, to, field, below, above, back_tables)
    returned = permutes(back_second, count)
    half = unpack_first(plan, to, back_first, expand)
    return unpack_second(plan, came, back_first, half, returned, expand)


def add_shifted(field, source, reach, side):
    count = field.shape[-1]
    node = np.arange(count)
    keep = side(node) & (node + reach >= 0) & (node + reach < count)
    pads = [(0, 0)] * (field.ndim - 1)
    if reach > 0:
        moved = jnp.pad(source[..., reach:], pads + [(0, reach)])
    else:
        moved = jnp.pad(source[..., :reach], pads + [(-reach, 0)])
    return field + jnp.where(jnp.asarray(keep), moved, 0.0)


def plain(plan, velocity, metric, mass_weights):
    count, square = plan.count, NP * NP
    synthesis, spanwise, analysis = (jnp.asarray(t, F32) for t in fourier_tables(plan.planes))
    slopes = gll_diff()
    group = plan.elements // count
    eye_elem, eye_side = np.eye(group), np.eye(NP)
    xi_matrix = jnp.asarray(np.kron(eye_elem, np.kron(eye_side, slopes.T)), F32)
    eta_matrix = jnp.asarray(np.kron(eye_elem, np.kron(slopes.T, eye_side)), F32)
    spread = lax.all_to_all(velocity, "fourier", split_axis=2, concat_axis=1, tiled=True)
    offset = lax.axis_index("fourier") * group * square
    factors = lax.dynamic_slice_in_dim(metric, offset, group * square, 1)
    weights = lax.dynamic_slice_in_dim(mass_weights, offset, group * square, 0)
    values = jnp.einsum("cmn,mz->czn", spread, synthesis, precision=HIGH)
    along_z = jnp.einsum("cmn,mz->czn", spread, spanwise, precision=HIGH)
    along_xi = jnp.einsum("czk,kn->czn", values, xi_matrix, precision=HIGH)
    along_eta = jnp.einsum("czk,kn->czn", values, eta_matrix, precision=HIGH)
    grad_x = factors[0] * along_xi + factors[2] * along_eta
    grad_y = factors[1] * along_xi + factors[3] * along_eta
    weighted = weights * (values[0] * grad_x + values[1] * grad_y + values[2] * along_z)
    coeffs = jnp.einsum("czn,mz->cmn", weighted, analysis, precision=HIGH)
    coeffs = lax.all_to_all(coeffs, "fourier", split_axis=1, concat_axis=2, tiled=True)
    last = NP - 1
    reach = square - last
    joined = add_shifted(coeffs, coeffs, reach, lambda n: n % NP == last)
    joined = add_shifted(joined, coeffs, -reach, lambda n: n % NP == 0)
    below, above = rim_exchange(joined, joined)
    result = add_shifted(joined, below, last * NP, lambda n: n % square < NP)
    return add_shifted(result, above, -last * NP, lambda n: n % square >= last * NP)


def shards(velocity, metric, mass_weights):
    plan = Plan(lax.axis_size("fourier"), velocity.shape[1], velocity.shape[2])
    step = chunked if plan.fits else plain
    return step(plan, velocity, metric, mass_weights)


def solution(mesh):
    in_specs = (P(None, "fourier", "elem"), P(None, "elem"), P("elem"))
    out_specs = P(None, "fourier", "elem")
    return jax.shard_map(shards, mesh=mesh, in_specs=in_specs, out_specs=out_specs, check_vma=False)
```

```python
import functools

import jax
import jax.numpy as jnp
import ml_dtypes
import numpy as np
from jax import lax
from jax.experimental import pallas as pl
from jax.experimental.pallas import tpu as pltpu
from jax.sharding import PartitionSpec as P

NP = 9
HIGH = lax.Precision.HIGHEST
BF = jnp.bfloat16
F32 = jnp.float32
LANES = 256
CHUNKS = 2
VMEM_LIMIT = 40 << 20


def gll_diff():
    half = [0.3631174638261782, 0.6771862795107377, 0.8997579954114602, 1.0]
    nodes = np.array([-v for v in half[::-1]] + [0.0] + half)
    points = nodes.shape[0]
    gaps = nodes[:, None] - nodes[None, :] + np.eye(points)
    bary = 1.0 / np.prod(gaps, axis=1)
    matrix = bary[None, :] / bary[:, None] / gaps
    matrix[np.arange(points), np.arange(points)] = 0.0
    matrix[np.arange(points), np.arange(points)] = -matrix.sum(axis=1)
    return matrix


def fourier_tables(planes):
    index = np.arange(planes)
    wave = (index + 1) // 2
    angles = 2.0 * np.pi * ((wave[:, None] * index[None, :]) % planes) / planes
    cosine_rows = ((index % 2 == 1) | (index == 0))[:, None]
    synthesis = np.where(cosine_rows, np.cos(angles), np.sin(angles))
    rate = wave * (8.0 / planes)
    rate[planes - 1] = 0.0
    spanwise = np.where(cosine_rows, -rate[:, None] * np.sin(angles), rate[:, None] * np.cos(angles))
    scale = np.where((index == 0) | (index == planes - 1), 1.0, 2.0) / planes
    analysis = synthesis * scale[:, None]
    return synthesis, spanwise, analysis


def halves(table):
    table = np.asarray(table, np.float32)
    high = table.astype(ml_dtypes.bfloat16)
    low = (table - high.astype(np.float32)).astype(ml_dtypes.bfloat16)
    return high, low


class Plan:
    def __init__(self, count, modes, nodes):
        self.count, self.modes, self.nodes = count, modes, nodes
        self.planes = count * modes
        self.elements = nodes // (NP * NP)
        self.main = modes // 16 * 16
        self.left = modes - self.main
        self.per_piece = self.elements // (count * CHUNKS)
        self.width = self.per_piece * NP * NP
        self.columns = self.per_piece * (NP - 1) + 1
        self.rows = 3 * self.main + 8
        self.pieces = CHUNKS * count
        self.joined = self.columns * NP
        self.stride = 14 * 128
        self.seam = -(-(count * self.width - self.width + NP * NP) // self.stride) * self.stride
        self.fits = (
            self.main > 0
            and 3 * self.left <= 8
            and self.elements % (count * CHUNKS) == 0
            and self.per_piece > 0
            and 128 < self.joined <= self.width <= LANES
            and self.seam <= count * self.width - NP * NP
            and self.columns <= 32
            and self.planes % 16 == 0
        )

    def lane(self, a, column):
        if column == 0:
            return a
        if column == self.columns - 1:
            return NP + a
        return 2 * NP + a * (self.columns - 2) + column - 1

    def tables(self):
        synthesis, spanwise, analysis = fourier_tables(self.planes)
        source = np.arange(self.count)
        main = (source[:, None] * self.modes + np.arange(self.main)[None, :]).reshape(-1)
        both = []
        for table in (synthesis, spanwise):
            high, low = halves(table.T[:, main])
            both.append(np.concatenate([high, high, low], axis=1))
        forward = np.stack(both)
        forward_left = np.zeros((3, 2, self.planes, 3 * 8 * self.count), ml_dtypes.bfloat16)
        back_left = np.zeros((3, 8 * self.count, 3 * self.planes), ml_dtypes.bfloat16)
        for c in range(3):
            for kind, table in enumerate((synthesis, spanwise)):
                wide = np.zeros((self.planes, 8 * self.count))
                for s in range(self.count):
                    for r in range(self.left):
                        wide[:, 8 * s + self.left * c + r] = table[s * self.modes + self.main + r]
                high, low = halves(wide)
                forward_left[c, kind] = np.concatenate([high, high, low], axis=1)
            tall = np.zeros((8 * self.count, self.planes))
            for s in range(self.count):
                for r in range(self.left):
                    tall[8 * s + self.left * c + r] = analysis[s * self.modes + self.main + r]
            high, low = halves(tall)
            back_left[c] = np.concatenate([high, high, low], axis=1)
        high, low = halves(analysis[main])
        back = np.concatenate([high, high, low], axis=1)
        return forward, forward_left, back, back_left

    def slopes(self):
        slopes = gll_diff()
        eye_elem, eye_side = np.eye(self.per_piece), np.eye(NP)
        wide = np.zeros((LANES, 2 * LANES))
        wide[: self.width, : self.width] = np.kron(eye_elem, np.kron(eye_side, slopes.T))
        wide[: self.width, LANES : LANES + self.width] = np.kron(eye_elem, np.kron(slopes.T, eye_side))
        high, low = halves(wide)
        return np.concatenate([high, high, low], axis=0)

    def assembly(self):
        join = np.zeros((3, LANES, 2 * LANES))
        rims = np.zeros((3, LANES, LANES))
        expand = np.zeros((LANES, LANES))
        for e in range(self.per_piece):
            for a in range(NP):
                for b in range(NP):
                    node, column = (e * NP + a) * NP + b, e * (NP - 1) + b
                    lane = self.lane(a, column)
                    expand[lane, node] = 1.0
                    for c in range(3):
                        join[c, node, lane] = 1.0
                        if a == 0:
                            join[c, node, LANES + 32 * c + column] = 1.0
                        if a == NP - 1:
                            join[c, node, LANES + 128 + 32 * c + column] = 1.0
        for c in range(3):
            for column in range(self.columns):
                rims[c, 32 * c + column, self.lane(0, column)] = 1.0
                rims[c, 128 + 32 * c + column, self.lane(NP - 1, column)] = 1.0
        kind = ml_dtypes.bfloat16
        join, rims, expand = join.astype(kind), rims.astype(kind), expand.astype(kind)
        return (
            np.concatenate([join, join], axis=1),
            np.concatenate([rims, rims], axis=1),
            np.concatenate([expand, expand], axis=0),
        )


def split(x):
    high = x.astype(BF)
    low = (x - high.astype(F32)).astype(BF)
    return high, low


def dot(a, b):
    return jnp.dot(a, b, preferred_element_type=F32)


def lane_ids():
    return lax.broadcasted_iota(jnp.int32, (8, 128), 1)


def put_rest(block, rest, rows, wide):
    lanes = lane_ids()
    count = -(-(rows // 8) * wide // 128)
    tiles = [None] * (count + 1)
    for t in range(rows // 8):
        tile, shift = t * wide // 128, t * wide % 128
        x = jnp.where(lanes < wide, rest[8 * t : 8 * t + 8, :], 0.0)
        if shift:
            x = pltpu.roll(x, shift, 1)
        parts = [(tile, jnp.where(lanes >= shift, x, 0.0) if shift else x)]
        if shift + wide > 128:
            parts.append((tile + 1, jnp.where(lanes < shift, x, 0.0)))
        for g, part in parts:
            tiles[g] = part if tiles[g] is None else tiles[g] + part
    for g in range(count):
        block[rows + 8 * g : rows + 8 * g + 8, :] = tiles[g]


def get_rest(block, t, rows, wide):
    lanes = lane_ids()
    tile, shift = t * wide // 128, t * wide % 128
    at = rows + 8 * tile
    x = block[at : at + 8, :]
    if shift + wide > 128:
        x = jnp.where(lanes >= shift, x, block[at + 8 : at + 16, :])
    return pltpu.roll(x, 128 - shift, 1) if shift else x


def wire_rows(rows, wide):
    return rows + 8 * (-(-(rows // 8) * wide // 128))


def by_step(steps, outs, buf):
    for s, out in enumerate(outs):
        out[...] = buf[steps[s]]


def pack_piece(plan, piece, v_ref, block, rest):
    start = piece * plan.width
    base = start // 128 * 128
    shift = start - base
    wide = LANES + 128
    tails = []
    for c in range(3):
        x = v_ref[c, : plan.main, base : base + wide]
        x = pltpu.roll(x, wide - shift, 1) if shift else x
        block[plan.main * c : plan.main * (c + 1), :] = x[:, :128]
        rest[plan.main * c : plan.main * (c + 1), :] = x[:, 128:LANES]
        if plan.left:
            tails.append(v_ref[c, plan.main : plan.modes, base : base + wide])
    tails.append(jnp.zeros((8 - 3 * plan.left, wide), F32))
    x = jnp.concatenate(tails, axis=0)
    x = pltpu.roll(x, wide - shift, 1) if shift else x
    block[3 * plan.main : plan.rows, :] = x[:, :128]
    rest[3 * plan.main : plan.rows, :] = x[:, 128:LANES]
    put_rest(block, rest, plan.rows, plan.width - 128)


def pack_first_kernel(plan, to_ref, v_ref, *refs):
    outs, (buf, rest) = refs[:-2], refs[-2:]
    for j in range(plan.count):
        pack_piece(plan, j, v_ref, buf.at[j], rest)
    by_step(to_ref, outs, buf)


def pack_second_kernel(plan, gate_ref, v_ref, out_ref, rest):
    for j in range(plan.count):
        pack_piece(plan, plan.count + j, v_ref, out_ref.at[j], rest)


def synth_kernel(plan, joined, from_ref, *refs):
    count, main = plan.count, plan.main
    blocks, refs = (refs[:1], refs[1:]) if joined else (refs[:count], refs[count:])
    t_ref, tl_ref, d_ref, join_ref, f_ref, w_ref, low_ref, up_ref, v3, raw, l3, u, dz = refs
    deep = main * count
    wide = plan.width - 128
    for s in range(count):
        source, block = (s, blocks[0].at[s]) if joined else (from_ref[s], blocks[s])
        at = source * main
        for c in range(3):
            rest = [get_rest(block, main // 8 * c + i, plan.rows, wide) for i in range(main // 8)]
            x = jnp.concatenate([block[main * c : main * (c + 1), :], jnp.concatenate(rest, axis=0)], axis=1)
            high, low = split(x)
            for i, part in enumerate((high, low, high)):
                where = i * deep + at
                v3[c, pl.ds(where if joined else pl.multiple_of(where, 16), main), :] = part
        rest = get_rest(block, 3 * main // 8, plan.rows, wide)
        where = source * 8
        x = jnp.concatenate([block[3 * main : plan.rows, :], rest], axis=1)
        raw[pl.ds(where if joined else pl.multiple_of(where, 8), 8), :] = x
    high, low = split(raw[...])
    l3[...] = jnp.concatenate([high, low, high], axis=0)

    @pl.loop(0, 3)
    def _(c):
        u[c] = dot(t_ref[0], v3[c]) + dot(tl_ref[c, 0], l3[...])
        dz[c] = dot(t_ref[1], v3[c]) + dot(tl_ref[c, 1], l3[...])

    low_ref[...] = jnp.zeros_like(low_ref)
    up_ref[...] = jnp.zeros_like(up_ref)

    @pl.loop(0, 3)
    def _(c):
        high, low = split(u[c])
        slope = dot(jnp.concatenate([high, low, high], axis=1), d_ref[...])
        along_xi, along_eta = slope[:, :LANES], slope[:, LANES:]
        grad_x = f_ref[0:1, :] * along_xi + f_ref[2:3, :] * along_eta
        grad_y = f_ref[1:2, :] * along_xi + f_ref[3:4, :] * along_eta
        weighted = f_ref[4:5, :] * (u[0] * grad_x + u[1] * grad_y + u[2] * dz[c])
        high, low = split(weighted)
        joined = dot(jnp.concatenate([high, low], axis=1), join_ref[c])
        w_ref[c] = joined[:, :LANES]
        low_ref[...] += joined[:, LANES : LANES + 128]
        up_ref[...] += joined[:, LANES + 128 :]


def analyse_kernel(plan, joined, to_ref, w_ref, below_ref, above_ref, a_ref, al_ref, rims_ref, *refs):
    outs, (w3, tail, rest) = (refs[:1], refs[1:]) if joined else (refs[: plan.count], refs[plan.count + 1 :])
    buf = outs[0] if joined else refs[plan.count]
    count, main = plan.count, plan.main
    high, low = split(jnp.concatenate([below_ref[...], above_ref[...]], axis=1))
    rims = jnp.concatenate([high, low], axis=1)
    tail[...] = jnp.zeros_like(tail)

    @pl.loop(0, 3)
    def _(c):
        high, low = split(w_ref[c] + dot(rims, rims_ref[c]))
        w3[...] = jnp.concatenate([high, low, high], axis=0)
        coeffs = dot(a_ref[...], w3[...])
        rows = pl.ds(pl.multiple_of(c * main, main), main)
        for d in range(count):
            buf[d, rows, :] = coeffs[main * d : main * (d + 1), :128]
            rest[d, rows, :] = coeffs[main * d : main * (d + 1), 128:]
        tail[...] += dot(al_ref[c], w3[...])

    for d in range(count):
        buf[d, 3 * main : plan.rows, :] = tail[8 * d : 8 * (d + 1), :128]
        rest[d, 3 * main : plan.rows, :] = tail[8 * d : 8 * (d + 1), 128:]
        put_rest(buf.at[d], rest.at[d], plan.rows, plan.joined - 128)
    if not joined:
        by_step(to_ref, outs, buf)


def unpack_lanes(plan, held, e_ref, lhs, grown, out_ref, base):
    rows, wide = plan.rows, plan.joined - 128
    pad = -(-rows // 16) * 16
    span = out_ref.shape[2]
    lanes = lax.broadcasted_iota(jnp.int32, (1, 128), 1)
    pieces = [i for i in range(plan.pieces) if i * plan.width < base + span and (i + 1) * plan.width > base]
    for n, i in enumerate(pieces):
        x = held[i][:rows, :]
        if i - 1 in held:
            x = x + jnp.where(lanes < NP, pltpu.roll(held[i - 1][:rows, :], 128 - NP, 1), 0.0)
        if i + 1 in held:
            inside = (lanes >= NP) & (lanes < 2 * NP)
            x = x + jnp.where(inside, pltpu.roll(held[i + 1][:rows, :], NP, 1), 0.0)
        rest = jnp.concatenate([get_rest(held[i], t, rows, wide) for t in range(rows // 8)], axis=0)
        x = jnp.concatenate([x, rest], axis=1)
        if pad > rows:
            x = jnp.concatenate([x, jnp.zeros((pad - rows, LANES), F32)], axis=0)
        high, low = split(x)
        lhs[pad * n : pad * (n + 1), :] = jnp.concatenate([high, low], axis=1)
    used = pad * len(pieces)
    grown[:used, :] = dot(lhs[:used, :], e_ref[...])
    tiles = {}
    for n, i in enumerate(pieces):
        for half in range(2):
            start = i * plan.width + 128 * half - base
            tile, shift = start // 128, start % 128
            x = grown[pad * n : pad * n + rows, 128 * half : 128 * (half + 1)]
            x = pltpu.roll(x, shift, 1) if shift else x
            tiles[tile] = jnp.where(lanes >= shift, x, tiles[tile]) if shift and tile in tiles else x
            if shift:
                tiles[tile + 1] = x
    for tile in range(span // 128):
        x = tiles.get(tile)
        if x is None:
            continue
        at = slice(128 * tile, 128 * (tile + 1))
        for c in range(3):
            out_ref[c, : plan.main, at] = x[plan.main * c : plan.main * (c + 1), :]
            if plan.left:
                row = 3 * plan.main + plan.left * c
                out_ref[c, plan.main :, at] = x[row : row + plan.left, :]


def unpack_first_kernel(plan, gate_ref, block_ref, e_ref, out_ref, lhs, grown):
    held = {i: block_ref.at[i] for i in range(plan.count)}
    unpack_lanes(plan, held, e_ref, lhs, grown, out_ref, 0)


def unpack_second_kernel(plan, steps, from_ref, before_ref, old_ref, e_ref, *refs):
    blocks, (out_ref, buf, lhs, grown) = refs[: plan.count], refs[plan.count :]
    step = pl.program_id(0)
    held = {plan.count + j: buf.at[j] for j in range(plan.count)}
    held[plan.count - 1] = before_ref.at[0]

    @pl.when(step == 0)
    def _():
        for s in range(plan.count):
            buf[from_ref[s]] = blocks[s][...]

    for i in range(steps):

        @pl.when(step == i)
        def _():
            unpack_lanes(plan, held, e_ref, lhs, grown, out_ref, plan.seam + i * plan.stride)


def smem():
    return pl.BlockSpec(memory_space=pltpu.SMEM)


def vmem():
    return pl.BlockSpec(memory_space=pltpu.VMEM)


def hbm():
    return pl.BlockSpec(memory_space=pl.ANY)


def params():
    return pltpu.CompilerParams(vmem_limit_bytes=VMEM_LIMIT)


def cost(flops, size):
    return pl.CostEstimate(flops=int(flops), bytes_accessed=int(size), transcendentals=0)


def pack_first(plan, to, velocity):
    last = (plan.count - 1) * plan.width
    reach = last // 128 * 128 + LANES + 128
    tall = wire_rows(plan.rows, plan.width - 128)
    return pl.pallas_call(
        functools.partial(pack_first_kernel, plan),
        in_specs=[smem(), vmem()],
        out_specs=[vmem()] * plan.count,
        out_shape=[jax.ShapeDtypeStruct((tall, 128), F32)] * plan.count,
        scratch_shapes=[pltpu.VMEM((plan.count, tall, 128), F32), pltpu.VMEM((plan.rows, 128), F32)],
        compiler_params=params(),
        cost_estimate=cost(0, 8 * plan.count * tall * 128),
        name="pack_first",
    )(to, lax.slice_in_dim(velocity, 0, reach, axis=2))


def pack_second(plan, gate, velocity):
    span = -(-plan.nodes // 128) * 128
    tall = wire_rows(plan.rows, plan.width - 128)
    return pl.pallas_call(
        functools.partial(pack_second_kernel, plan),
        grid=(1,),
        in_specs=[smem(), pl.BlockSpec((3, plan.modes, span), lambda i: (0, 0, 0))],
        out_specs=pl.BlockSpec((plan.count, tall, 128), lambda i: (0, 0, 0)),
        out_shape=jax.ShapeDtypeStruct((plan.count, tall, 128), F32),
        scratch_shapes=[pltpu.VMEM((plan.rows, 128), F32)],
        compiler_params=params(),
        cost_estimate=cost(0, 8 * plan.count * tall * 128),
        name="pack_second",
    )(gate, velocity)


def synth(plan, name, came, blocks, tables, factors):
    joined = not isinstance(blocks, list)
    blocks = [blocks] if joined else blocks
    deep = plan.main * plan.count
    small = 8 * plan.count
    field = jax.ShapeDtypeStruct((3, plan.planes, LANES), F32)
    rim = jax.ShapeDtypeStruct((plan.planes, 128), F32)
    return pl.pallas_call(
        functools.partial(synth_kernel, plan, joined),
        in_specs=[smem()] + [vmem()] * (len(blocks) + 5),
        out_specs=[vmem()] * 3,
        out_shape=[field, rim, rim],
        scratch_shapes=[
            pltpu.VMEM((3, 3 * deep, LANES), BF),
            pltpu.VMEM((small, LANES), F32),
            pltpu.VMEM((3 * small, LANES), BF),
            pltpu.VMEM((3, plan.planes, LANES), F32),
            pltpu.VMEM((3, plan.planes, LANES), F32),
        ],
        compiler_params=params(),
        cost_estimate=cost(3 * 2 * plan.planes * LANES * (6 * deep + 6 * LANES + 4 * LANES), 12 << 20),
        name=name,
    )(came, *blocks, *tables, factors)


def analyse(plan, name, joined, to, field, below, above, tables):
    count = plan.count
    tall = wire_rows(plan.rows, plan.joined - 128)
    if joined:
        shape, specs, extra = jax.ShapeDtypeStruct((count, tall, 128), F32), vmem(), []
    else:
        shape, specs = [jax.ShapeDtypeStruct((tall, 128), F32)] * count, [vmem()] * count
        extra = [pltpu.VMEM((count, tall, 128), F32)]
    return pl.pallas_call(
        functools.partial(analyse_kernel, plan, joined),
        in_specs=[smem()] + [vmem()] * 6,
        out_specs=specs,
        out_shape=shape,
        scratch_shapes=extra
        + [
            pltpu.VMEM((3 * plan.planes, LANES), BF),
            pltpu.VMEM((8 * count, LANES), F32),
            pltpu.VMEM((count, plan.rows, 128), F32),
        ],
        compiler_params=params(),
        cost_estimate=cost(3 * 2 * plan.planes * LANES * 3 * plan.planes, 6 << 20),
        name=name,
    )(to, field, below, above, *tables)


def unpack_scratch(plan, span):
    pieces = min(plan.pieces, -(-span // plan.width) + 1)
    pad = -(-plan.rows // 16) * 16
    return [pltpu.VMEM((pieces * pad, 2 * LANES), BF), pltpu.VMEM((pieces * pad, LANES), F32)]


def unpack_first(plan, gate, blocks, expand):
    out = jax.ShapeDtypeStruct((3, plan.modes, plan.nodes), F32)
    return pl.pallas_call(
        functools.partial(unpack_first_kernel, plan),
        grid=(1,),
        in_specs=[smem(), vmem(), vmem()],
        out_specs=pl.BlockSpec((3, plan.modes, plan.seam), lambda i: (0, 0, 0)),
        out_shape=out,
        scratch_shapes=unpack_scratch(plan, plan.seam),
        compiler_params=params(),
        cost_estimate=cost(2 * plan.count * plan.rows * LANES * 2 * LANES, 4 << 20),
        name="unpack_first",
    )(gate, blocks, expand)


def unpack_second(plan, came, before, old, blocks, expand):
    tall = blocks[0].shape[0]
    steps = -(-(plan.nodes - plan.seam) // plan.stride)
    skip = plan.seam // plan.stride
    return pl.pallas_call(
        functools.partial(unpack_second_kernel, plan, steps),
        grid=(steps,),
        in_specs=[
            smem(),
            pl.BlockSpec((1, tall, 128), lambda i: (plan.count - 1, 0, 0)),
            hbm(),
            pl.BlockSpec(expand.shape, lambda i: (0, 0)),
        ]
        + [pl.BlockSpec((tall, 128), lambda i: (0, 0))] * plan.count,
        out_specs=pl.BlockSpec((3, plan.modes, plan.stride), lambda i: (0, 0, i + skip)),
        out_shape=jax.ShapeDtypeStruct((3, plan.modes, plan.nodes), F32),
        scratch_shapes=[pltpu.VMEM((plan.count, tall, 128), F32)] + unpack_scratch(plan, plan.stride),
        input_output_aliases={2: 0},
        compiler_params=params(),
        cost_estimate=cost(2 * plan.count * plan.rows * LANES * 2 * LANES, 4 << 20),
        name="unpack_second",
    )(came, before, old, expand, *blocks)


def permutes(blocks, count):
    outs = [blocks[0]]
    for s in range(1, count):
        outs.append(lax.ppermute(blocks[s], "fourier", [(k, (k + s) % count) for k in range(count)]))
    return outs


def all_at_once(blocks):
    return lax.all_to_all(blocks, "fourier", split_axis=0, concat_axis=0, tiled=True)


def rim_exchange(low, up):
    ends = lax.axis_size("elem") - 1
    below = lax.ppermute(up, "elem", [(i, i + 1) for i in range(ends)])
    above = lax.ppermute(low, "elem", [(i + 1, i) for i in range(ends)])
    return below, above


def after(x, other):
    return lax.optimization_barrier((x, other))[0]


def chunked(plan, velocity, metric, mass_weights):
    count = plan.count
    here = lax.axis_index("fourier").astype(jnp.int32)
    steps = jnp.arange(count, dtype=jnp.int32)
    to, came = (here + steps) % count, (here - steps + count) % count
    forward, forward_left, back, back_left = (jnp.asarray(t) for t in plan.tables())
    slopes = jnp.asarray(plan.slopes())
    join, rims, expand = (jnp.asarray(t) for t in plan.assembly())
    local = jnp.concatenate([metric, mass_weights[None], jnp.zeros((3, plan.nodes), F32)], axis=0)
    tables = (forward, forward_left, slopes, join)
    back_tables = (back, back_left, rims)
    factors = []
    for q in range(CHUNKS):
        start = (here + q * count) * plan.width
        cut = lax.dynamic_slice_in_dim(local, start, plan.width, 1)
        factors.append(jnp.pad(cut, ((0, 0), (0, LANES - plan.width))))

    sent = pack_first(plan, to, velocity)
    spread = permutes(sent, count)
    second = pack_second(plan, after(to, sent[1]), velocity)
    second = all_at_once(after(second, spread))
    field, low, up = synth(plan, "synth_first", came, spread, tables, factors[0])
    below, above = rim_exchange(low, up)
    back_first = analyse(plan, "analyse_first", True, to, field, below, above, back_tables)
    back_first = all_at_once(after(back_first, second))
    field, low, up = synth(plan, "synth_second", came, second, tables, factors[1])
    below, above = rim_exchange(low, up)
    back_second = analyse(plan, "analyse_second", False, to, field, below, above, back_tables)
    returned = permutes(back_second, count)
    half = unpack_first(plan, to, back_first, expand)
    return unpack_second(plan, came, back_first, half, returned, expand)


def add_shifted(field, source, reach, side):
    count = field.shape[-1]
    node = np.arange(count)
    keep = side(node) & (node + reach >= 0) & (node + reach < count)
    pads = [(0, 0)] * (field.ndim - 1)
    if reach > 0:
        moved = jnp.pad(source[..., reach:], pads + [(0, reach)])
    else:
        moved = jnp.pad(source[..., :reach], pads + [(-reach, 0)])
    return field + jnp.where(jnp.asarray(keep), moved, 0.0)


def plain(plan, velocity, metric, mass_weights):
    count, square = plan.count, NP * NP
    synthesis, spanwise, analysis = (jnp.asarray(t, F32) for t in fourier_tables(plan.planes))
    slopes = gll_diff()
    group = plan.elements // count
    eye_elem, eye_side = np.eye(group), np.eye(NP)
    xi_matrix = jnp.asarray(np.kron(eye_elem, np.kron(eye_side, slopes.T)), F32)
    eta_matrix = jnp.asarray(np.kron(eye_elem, np.kron(slopes.T, eye_side)), F32)
    spread = lax.all_to_all(velocity, "fourier", split_axis=2, concat_axis=1, tiled=True)
    offset = lax.axis_index("fourier") * group * square
    factors = lax.dynamic_slice_in_dim(metric, offset, group * square, 1)
    weights = lax.dynamic_slice_in_dim(mass_weights, offset, group * square, 0)
    values = jnp.einsum("cmn,mz->czn", spread, synthesis, precision=HIGH)
    along_z = jnp.einsum("cmn,mz->czn", spread, spanwise, precision=HIGH)
    along_xi = jnp.einsum("czk,kn->czn", values, xi_matrix, precision=HIGH)
    along_eta = jnp.einsum("czk,kn->czn", values, eta_matrix, precision=HIGH)
    grad_x = factors[0] * along_xi + factors[2] * along_eta
    grad_y = factors[1] * along_xi + factors[3] * along_eta
    weighted = weights * (values[0] * grad_x + values[1] * grad_y + values[2] * along_z)
    coeffs = jnp.einsum("czn,mz->cmn", weighted, analysis, precision=HIGH)
    coeffs = lax.all_to_all(coeffs, "fourier", split_axis=1, concat_axis=2, tiled=True)
    last = NP - 1
    reach = square - last
    joined = add_shifted(coeffs, coeffs, reach, lambda n: n % NP == last)
    joined = add_shifted(joined, coeffs, -reach, lambda n: n % NP == 0)
    below, above = rim_exchange(joined, joined)
    result = add_shifted(joined, below, last * NP, lambda n: n % square < NP)
    return add_shifted(result, above, -last * NP, lambda n: n % square >= last * NP)


def shards(velocity, metric, mass_weights):
    plan = Plan(lax.axis_size("fourier"), velocity.shape[1], velocity.shape[2])
    step = chunked if plan.fits else plain
    return step(plan, velocity, metric, mass_weights)


def solution(mesh):
    in_specs = (P(None, "fourier", "elem"), P(None, "elem"), P("elem"))
    out_specs = P(None, "fourier", "elem")
    return jax.shard_map(shards, mesh=mesh, in_specs=in_specs, out_specs=out_specs, check_vma=False)
```

```python
import functools

import jax
import jax.numpy as jnp
import ml_dtypes
import numpy as np
from jax import lax
from jax.experimental import pallas as pl
from jax.experimental.pallas import tpu as pltpu
from jax.sharding import PartitionSpec as P

NP = 9
HIGH = lax.Precision.HIGHEST
BF = jnp.bfloat16
F32 = jnp.float32
LANES = 256
CHUNKS = 2
VMEM_LIMIT = 40 << 20


def gll_diff():
    half = [0.3631174638261782, 0.6771862795107377, 0.8997579954114602, 1.0]
    nodes = np.array([-v for v in half[::-1]] + [0.0] + half)
    points = nodes.shape[0]
    gaps = nodes[:, None] - nodes[None, :] + np.eye(points)
    bary = 1.0 / np.prod(gaps, axis=1)
    matrix = bary[None, :] / bary[:, None] / gaps
    matrix[np.arange(points), np.arange(points)] = 0.0
    matrix[np.arange(points), np.arange(points)] = -matrix.sum(axis=1)
    return matrix


def fourier_tables(planes):
    index = np.arange(planes)
    wave = (index + 1) // 2
    angles = 2.0 * np.pi * ((wave[:, None] * index[None, :]) % planes) / planes
    cosine_rows = ((index % 2 == 1) | (index == 0))[:, None]
    synthesis = np.where(cosine_rows, np.cos(angles), np.sin(angles))
    rate = wave * (8.0 / planes)
    rate[planes - 1] = 0.0
    spanwise = np.where(cosine_rows, -rate[:, None] * np.sin(angles), rate[:, None] * np.cos(angles))
    scale = np.where((index == 0) | (index == planes - 1), 1.0, 2.0) / planes
    analysis = synthesis * scale[:, None]
    return synthesis, spanwise, analysis


def halves(table):
    table = np.asarray(table, np.float32)
    high = table.astype(ml_dtypes.bfloat16)
    low = (table - high.astype(np.float32)).astype(ml_dtypes.bfloat16)
    return high, low


class Plan:
    def __init__(self, count, modes, nodes):
        self.count, self.modes, self.nodes = count, modes, nodes
        self.planes = count * modes
        self.elements = nodes // (NP * NP)
        self.main = modes // 16 * 16
        self.left = modes - self.main
        self.per_piece = self.elements // (count * CHUNKS)
        self.width = self.per_piece * NP * NP
        self.columns = self.per_piece * (NP - 1) + 1
        self.rows = 3 * self.main + 8
        self.pieces = CHUNKS * count
        self.joined = self.columns * NP
        self.stride = 14 * 128
        self.seam = -(-(count * self.width - self.width + NP * NP) // self.stride) * self.stride
        self.fits = (
            self.main > 0
            and 3 * self.left <= 8
            and self.elements % (count * CHUNKS) == 0
            and self.per_piece > 0
            and 128 < self.joined <= self.width <= LANES
            and self.seam <= count * self.width - NP * NP
            and self.columns <= 32
            and self.planes % 16 == 0
        )

    def lane(self, a, column):
        if column == 0:
            return a
        if column == self.columns - 1:
            return NP + a
        return 2 * NP + a * (self.columns - 2) + column - 1

    def tables(self):
        synthesis, spanwise, analysis = fourier_tables(self.planes)
        source = np.arange(self.count)
        main = (source[:, None] * self.modes + np.arange(self.main)[None, :]).reshape(-1)
        both = []
        for table in (synthesis, spanwise):
            high, low = halves(table.T[:, main])
            both.append(np.concatenate([high, high, low], axis=1))
        forward = np.stack(both)
        forward_left = np.zeros((3, 2, self.planes, 3 * 8 * self.count), ml_dtypes.bfloat16)
        back_left = np.zeros((3, 8 * self.count, 3 * self.planes), ml_dtypes.bfloat16)
        for c in range(3):
            for kind, table in enumerate((synthesis, spanwise)):
                wide = np.zeros((self.planes, 8 * self.count))
                for s in range(self.count):
                    for r in range(self.left):
                        wide[:, 8 * s + self.left * c + r] = table[s * self.modes + self.main + r]
                high, low = halves(wide)
                forward_left[c, kind] = np.concatenate([high, high, low], axis=1)
            tall = np.zeros((8 * self.count, self.planes))
            for s in range(self.count):
                for r in range(self.left):
                    tall[8 * s + self.left * c + r] = analysis[s * self.modes + self.main + r]
            high, low = halves(tall)
            back_left[c] = np.concatenate([high, high, low], axis=1)
        high, low = halves(analysis[main])
        back = np.concatenate([high, high, low], axis=1)
        return forward, forward_left, back, back_left

    def slopes(self):
        slopes = gll_diff()
        eye_elem, eye_side = np.eye(self.per_piece), np.eye(NP)
        wide = np.zeros((LANES, 2 * LANES))
        wide[: self.width, : self.width] = np.kron(eye_elem, np.kron(eye_side, slopes.T))
        wide[: self.width, LANES : LANES + self.width] = np.kron(eye_elem, np.kron(slopes.T, eye_side))
        high, low = halves(wide)
        return np.concatenate([high, high, low], axis=0)

    def assembly(self):
        join = np.zeros((3, LANES, 2 * LANES))
        rims = np.zeros((3, LANES, LANES))
        expand = np.zeros((LANES, LANES))
        for e in range(self.per_piece):
            for a in range(NP):
                for b in range(NP):
                    node, column = (e * NP + a) * NP + b, e * (NP - 1) + b
                    lane = self.lane(a, column)
                    expand[lane, node] = 1.0
                    for c in range(3):
                        join[c, node, lane] = 1.0
                        if a == 0:
                            join[c, node, LANES + 32 * c + column] = 1.0
                        if a == NP - 1:
                            join[c, node, LANES + 128 + 32 * c + column] = 1.0
        for c in range(3):
            for column in range(self.columns):
                rims[c, 32 * c + column, self.lane(0, column)] = 1.0
                rims[c, 128 + 32 * c + column, self.lane(NP - 1, column)] = 1.0
        kind = ml_dtypes.bfloat16
        join, rims, expand = join.astype(kind), rims.astype(kind), expand.astype(kind)
        return (
            np.concatenate([join, join], axis=1),
            np.concatenate([rims, rims], axis=1),
            np.concatenate([expand, expand], axis=0),
        )


def split(x):
    high = x.astype(BF)
    low = (x - high.astype(F32)).astype(BF)
    return high, low


def dot(a, b):
    return jnp.dot(a, b, preferred_element_type=F32)


def lane_ids():
    return lax.broadcasted_iota(jnp.int32, (8, 128), 1)


def put_rest(block, rest, rows, wide):
    lanes = lane_ids()
    count = -(-(rows // 8) * wide // 128)
    tiles = [None] * (count + 1)
    for t in range(rows // 8):
        tile, shift = t * wide // 128, t * wide % 128
        x = jnp.where(lanes < wide, rest[8 * t : 8 * t + 8, :], 0.0)
        if shift:
            x = pltpu.roll(x, shift, 1)
        parts = [(tile, jnp.where(lanes >= shift, x, 0.0) if shift else x)]
        if shift + wide > 128:
            parts.append((tile + 1, jnp.where(lanes < shift, x, 0.0)))
        for g, part in parts:
            tiles[g] = part if tiles[g] is None else tiles[g] + part
    for g in range(count):
        block[rows + 8 * g : rows + 8 * g + 8, :] = tiles[g]


def get_rest(block, t, rows, wide):
    lanes = lane_ids()
    tile, shift = t * wide // 128, t * wide % 128
    at = rows + 8 * tile
    x = block[at : at + 8, :]
    if shift + wide > 128:
        x = jnp.where(lanes >= shift, x, block[at + 8 : at + 16, :])
    return pltpu.roll(x, 128 - shift, 1) if shift else x


def wire_rows(rows, wide):
    return rows + 8 * (-(-(rows // 8) * wide // 128))


def by_step(steps, outs, buf):
    for s, out in enumerate(outs):
        out[...] = buf[steps[s]]


def pack_part(plan, piece, c, v_ref, block, rest):
    start = piece * plan.width
    base, shift = start // 128 * 128, start % 128
    wide = LANES + 128
    rows = slice(plan.main * c, plan.main * (c + 1))
    x = v_ref[c, : plan.main, base : base + wide]
    x = pltpu.roll(x, wide - shift, 1) if shift else x
    block[rows, :] = x[:, :128]
    rest[rows, :] = x[:, 128:LANES]


def pack_tail(plan, piece, v_ref, block, rest):
    start = piece * plan.width
    base, shift = start // 128 * 128, start % 128
    wide = LANES + 128
    tails = [v_ref[c, plan.main : plan.modes, base : base + wide] for c in range(3) if plan.left]
    tails.append(jnp.zeros((8 - 3 * plan.left, wide), F32))
    x = jnp.concatenate(tails, axis=0)
    x = pltpu.roll(x, wide - shift, 1) if shift else x
    block[3 * plan.main : plan.rows, :] = x[:, :128]
    rest[3 * plan.main : plan.rows, :] = x[:, 128:LANES]
    put_rest(block, rest, plan.rows, plan.width - 128)


def pack_first_kernel(plan, to_ref, v_hbm, *refs):
    outs, (held, buf, rest, sems) = refs[:-4], refs[-4:]
    reach = held.shape[2]
    copies = [
        pltpu.make_async_copy(v_hbm.at[c, :, pl.ds(0, reach)], held.at[c], sems.at[c]) for c in range(3)
    ]
    for copy in copies:
        copy.start()
    for c in range(3):
        copies[c].wait()
        for j in range(plan.count):
            pack_part(plan, j, c, held, buf.at[j], rest.at[j])
    for j in range(plan.count):
        pack_tail(plan, j, held, buf.at[j], rest.at[j])
    by_step(to_ref, outs, buf)


def pack_second_kernel(plan, gate_ref, v_ref, out_ref, rest):
    for j in range(plan.count):
        for c in range(3):
            pack_part(plan, plan.count + j, c, v_ref, out_ref.at[j], rest)
        pack_tail(plan, plan.count + j, v_ref, out_ref.at[j], rest)


def synth_kernel(plan, joined, from_ref, *refs):
    count, main = plan.count, plan.main
    blocks, refs = (refs[:1], refs[1:]) if joined else (refs[:count], refs[count:])
    t_ref, tl_ref, d_ref, join_ref, f_ref, w_ref, low_ref, up_ref, v3, raw, l3, u, dz = refs
    deep = main * count
    wide = plan.width - 128
    for s in range(count):
        source, block = (s, blocks[0].at[s]) if joined else (from_ref[s], blocks[s])
        at = source * main
        for c in range(3):
            rest = [get_rest(block, main // 8 * c + i, plan.rows, wide) for i in range(main // 8)]
            x = jnp.concatenate([block[main * c : main * (c + 1), :], jnp.concatenate(rest, axis=0)], axis=1)
            high, low = split(x)
            for i, part in enumerate((high, low, high)):
                where = i * deep + at
                v3[c, pl.ds(where if joined else pl.multiple_of(where, 16), main), :] = part
        rest = get_rest(block, 3 * main // 8, plan.rows, wide)
        where = source * 8
        x = jnp.concatenate([block[3 * main : plan.rows, :], rest], axis=1)
        raw[pl.ds(where if joined else pl.multiple_of(where, 8), 8), :] = x
    high, low = split(raw[...])
    l3[...] = jnp.concatenate([high, low, high], axis=0)

    @pl.loop(0, 3)
    def _(c):
        u[c] = dot(t_ref[0], v3[c]) + dot(tl_ref[c, 0], l3[...])
        dz[c] = dot(t_ref[1], v3[c]) + dot(tl_ref[c, 1], l3[...])

    low_ref[...] = jnp.zeros_like(low_ref)
    up_ref[...] = jnp.zeros_like(up_ref)

    @pl.loop(0, 3)
    def _(c):
        high, low = split(u[c])
        slope = dot(jnp.concatenate([high, low, high], axis=1), d_ref[...])
        along_xi, along_eta = slope[:, :LANES], slope[:, LANES:]
        grad_x = f_ref[0:1, :] * along_xi + f_ref[2:3, :] * along_eta
        grad_y = f_ref[1:2, :] * along_xi + f_ref[3:4, :] * along_eta
        weighted = f_ref[4:5, :] * (u[0] * grad_x + u[1] * grad_y + u[2] * dz[c])
        high, low = split(weighted)
        joined = dot(jnp.concatenate([high, low], axis=1), join_ref[c])
        w_ref[c] = joined[:, :LANES]
        low_ref[...] += joined[:, LANES : LANES + 128]
        up_ref[...] += joined[:, LANES + 128 :]


def analyse_kernel(plan, joined, to_ref, w_ref, below_ref, above_ref, a_ref, al_ref, rims_ref, *refs):
    outs, (w3, tail, rest) = (refs[:1], refs[1:]) if joined else (refs[: plan.count], refs[plan.count + 1 :])
    buf = outs[0] if joined else refs[plan.count]
    count, main = plan.count, plan.main
    high, low = split(jnp.concatenate([below_ref[...], above_ref[...]], axis=1))
    rims = jnp.concatenate([high, low], axis=1)
    tail[...] = jnp.zeros_like(tail)

    @pl.loop(0, 3)
    def _(c):
        high, low = split(w_ref[c] + dot(rims, rims_ref[c]))
        w3[...] = jnp.concatenate([high, low, high], axis=0)
        coeffs = dot(a_ref[...], w3[...])
        rows = pl.ds(pl.multiple_of(c * main, main), main)
        for d in range(count):
            buf[d, rows, :] = coeffs[main * d : main * (d + 1), :128]
            rest[d, rows, :] = coeffs[main * d : main * (d + 1), 128:]
        tail[...] += dot(al_ref[c], w3[...])

    for d in range(count):
        buf[d, 3 * main : plan.rows, :] = tail[8 * d : 8 * (d + 1), :128]
        rest[d, 3 * main : plan.rows, :] = tail[8 * d : 8 * (d + 1), 128:]
        put_rest(buf.at[d], rest.at[d], plan.rows, plan.joined - 128)
    if not joined:
        by_step(to_ref, outs, buf)


def unpack_lanes(plan, held, e_ref, lhs, grown, out_ref, base):
    rows, wide = plan.rows, plan.joined - 128
    pad = -(-rows // 16) * 16
    span = out_ref.shape[2]
    lanes = lax.broadcasted_iota(jnp.int32, (1, 128), 1)
    pieces = [i for i in range(plan.pieces) if i * plan.width < base + span and (i + 1) * plan.width > base]
    for n, i in enumerate(pieces):
        x = held[i][:rows, :]
        if i - 1 in held:
            x = x + jnp.where(lanes < NP, pltpu.roll(held[i - 1][:rows, :], 128 - NP, 1), 0.0)
        if i + 1 in held:
            inside = (lanes >= NP) & (lanes < 2 * NP)
            x = x + jnp.where(inside, pltpu.roll(held[i + 1][:rows, :], NP, 1), 0.0)
        rest = jnp.concatenate([get_rest(held[i], t, rows, wide) for t in range(rows // 8)], axis=0)
        x = jnp.concatenate([x, rest], axis=1)
        if pad > rows:
            x = jnp.concatenate([x, jnp.zeros((pad - rows, LANES), F32)], axis=0)
        high, low = split(x)
        lhs[pad * n : pad * (n + 1), :] = jnp.concatenate([high, low], axis=1)
    used = pad * len(pieces)
    grown[:used, :] = dot(lhs[:used, :], e_ref[...])
    tiles = {}
    for n, i in enumerate(pieces):
        for half in range(2):
            start = i * plan.width + 128 * half - base
            tile, shift = start // 128, start % 128
            x = grown[pad * n : pad * n + rows, 128 * half : 128 * (half + 1)]
            x = pltpu.roll(x, shift, 1) if shift else x
            tiles[tile] = jnp.where(lanes >= shift, x, tiles[tile]) if shift and tile in tiles else x
            if shift:
                tiles[tile + 1] = x
    for tile in range(span // 128):
        x = tiles.get(tile)
        if x is None:
            continue
        at = slice(128 * tile, 128 * (tile + 1))
        for c in range(3):
            out_ref[c, : plan.main, at] = x[plan.main * c : plan.main * (c + 1), :]
            if plan.left:
                row = 3 * plan.main + plan.left * c
                out_ref[c, plan.main :, at] = x[row : row + plan.left, :]


def unpack_first_kernel(plan, gate_ref, block_ref, e_ref, out_ref, lhs, grown):
    held = {i: block_ref.at[i] for i in range(plan.count)}
    unpack_lanes(plan, held, e_ref, lhs, grown, out_ref, 0)


def unpack_second_kernel(plan, steps, from_ref, before_ref, old_ref, e_ref, *refs):
    blocks, (out_ref, buf, lhs, grown) = refs[: plan.count], refs[plan.count :]
    step = pl.program_id(0)
    held = {plan.count + j: buf.at[j] for j in range(plan.count)}
    held[plan.count - 1] = before_ref.at[0]

    @pl.when(step == 0)
    def _():
        for s in range(plan.count):
            buf[from_ref[s]] = blocks[s][...]

    for i in range(steps):

        @pl.when(step == i)
        def _():
            unpack_lanes(plan, held, e_ref, lhs, grown, out_ref, plan.seam + i * plan.stride)


def smem():
    return pl.BlockSpec(memory_space=pltpu.SMEM)


def vmem():
    return pl.BlockSpec(memory_space=pltpu.VMEM)


def hbm():
    return pl.BlockSpec(memory_space=pl.ANY)


def params():
    return pltpu.CompilerParams(vmem_limit_bytes=VMEM_LIMIT)


def cost(flops, size):
    return pl.CostEstimate(flops=int(flops), bytes_accessed=int(size), transcendentals=0)


def pack_first(plan, to, velocity):
    last = (plan.count - 1) * plan.width
    reach = last // 128 * 128 + LANES + 128
    tall = wire_rows(plan.rows, plan.width - 128)
    return pl.pallas_call(
        functools.partial(pack_first_kernel, plan),
        in_specs=[smem(), pl.BlockSpec(memory_space=pltpu.MemorySpace.HBM)],
        out_specs=[vmem()] * plan.count,
        out_shape=[jax.ShapeDtypeStruct((tall, 128), F32)] * plan.count,
        scratch_shapes=[
            pltpu.VMEM((3, plan.modes, reach), F32),
            pltpu.VMEM((plan.count, tall, 128), F32),
            pltpu.VMEM((plan.count, plan.rows, 128), F32),
            pltpu.SemaphoreType.DMA((3,)),
        ],
        compiler_params=params(),
        cost_estimate=cost(0, 8 * plan.count * tall * 128),
        name="pack_first",
    )(to, pltpu.with_memory_space_constraint(velocity, pltpu.MemorySpace.HBM))


def pack_second(plan, gate, velocity):
    span = -(-plan.nodes // 128) * 128
    tall = wire_rows(plan.rows, plan.width - 128)
    return pl.pallas_call(
        functools.partial(pack_second_kernel, plan),
        grid=(1,),
        in_specs=[smem(), pl.BlockSpec((3, plan.modes, span), lambda i: (0, 0, 0))],
        out_specs=pl.BlockSpec((plan.count, tall, 128), lambda i: (0, 0, 0)),
        out_shape=jax.ShapeDtypeStruct((plan.count, tall, 128), F32),
        scratch_shapes=[pltpu.VMEM((plan.rows, 128), F32)],
        compiler_params=params(),
        cost_estimate=cost(0, 8 * plan.count * tall * 128),
        name="pack_second",
    )(gate, pltpu.with_memory_space_constraint(velocity, pltpu.MemorySpace.HBM))


def synth(plan, name, came, blocks, tables, factors):
    joined = not isinstance(blocks, list)
    blocks = [blocks] if joined else blocks
    deep = plan.main * plan.count
    small = 8 * plan.count
    field = jax.ShapeDtypeStruct((3, plan.planes, LANES), F32)
    rim = jax.ShapeDtypeStruct((plan.planes, 128), F32)
    return pl.pallas_call(
        functools.partial(synth_kernel, plan, joined),
        in_specs=[smem()] + [vmem()] * (len(blocks) + 5),
        out_specs=[vmem()] * 3,
        out_shape=[field, rim, rim],
        scratch_shapes=[
            pltpu.VMEM((3, 3 * deep, LANES), BF),
            pltpu.VMEM((small, LANES), F32),
            pltpu.VMEM((3 * small, LANES), BF),
            pltpu.VMEM((3, plan.planes, LANES), F32),
            pltpu.VMEM((3, plan.planes, LANES), F32),
        ],
        compiler_params=params(),
        cost_estimate=cost(3 * 2 * plan.planes * LANES * (6 * deep + 6 * LANES + 4 * LANES), 12 << 20),
        name=name,
    )(came, *blocks, *tables, factors)


def analyse(plan, name, joined, to, field, below, above, tables):
    count = plan.count
    tall = wire_rows(plan.rows, plan.joined - 128)
    if joined:
        shape, specs, extra = jax.ShapeDtypeStruct((count, tall, 128), F32), vmem(), []
    else:
        shape, specs = [jax.ShapeDtypeStruct((tall, 128), F32)] * count, [vmem()] * count
        extra = [pltpu.VMEM((count, tall, 128), F32)]
    return pl.pallas_call(
        functools.partial(analyse_kernel, plan, joined),
        in_specs=[smem()] + [vmem()] * 6,
        out_specs=specs,
        out_shape=shape,
        scratch_shapes=extra
        + [
            pltpu.VMEM((3 * plan.planes, LANES), BF),
            pltpu.VMEM((8 * count, LANES), F32),
            pltpu.VMEM((count, plan.rows, 128), F32),
        ],
        compiler_params=params(),
        cost_estimate=cost(3 * 2 * plan.planes * LANES * 3 * plan.planes, 6 << 20),
        name=name,
    )(to, field, below, above, *tables)


def unpack_scratch(plan, span):
    pieces = min(plan.pieces, -(-span // plan.width) + 1)
    pad = -(-plan.rows // 16) * 16
    return [pltpu.VMEM((pieces * pad, 2 * LANES), BF), pltpu.VMEM((pieces * pad, LANES), F32)]


def unpack_first(plan, gate, blocks, expand):
    out = jax.ShapeDtypeStruct((3, plan.modes, plan.nodes), F32)
    return pl.pallas_call(
        functools.partial(unpack_first_kernel, plan),
        grid=(1,),
        in_specs=[smem(), vmem(), vmem()],
        out_specs=pl.BlockSpec((3, plan.modes, plan.seam), lambda i: (0, 0, 0)),
        out_shape=out,
        scratch_shapes=unpack_scratch(plan, plan.seam),
        compiler_params=params(),
        cost_estimate=cost(2 * plan.count * plan.rows * LANES * 2 * LANES, 4 << 20),
        name="unpack_first",
    )(gate, blocks, expand)


def unpack_second(plan, came, before, old, blocks, expand):
    tall = blocks[0].shape[0]
    steps = -(-(plan.nodes - plan.seam) // plan.stride)
    skip = plan.seam // plan.stride
    return pl.pallas_call(
        functools.partial(unpack_second_kernel, plan, steps),
        grid=(steps,),
        in_specs=[
            smem(),
            pl.BlockSpec((1, tall, 128), lambda i: (plan.count - 1, 0, 0)),
            hbm(),
            pl.BlockSpec(expand.shape, lambda i: (0, 0)),
        ]
        + [pl.BlockSpec((tall, 128), lambda i: (0, 0))] * plan.count,
        out_specs=pl.BlockSpec((3, plan.modes, plan.stride), lambda i: (0, 0, i + skip)),
        out_shape=jax.ShapeDtypeStruct((3, plan.modes, plan.nodes), F32),
        scratch_shapes=[pltpu.VMEM((plan.count, tall, 128), F32)] + unpack_scratch(plan, plan.stride),
        input_output_aliases={2: 0},
        compiler_params=params(),
        cost_estimate=cost(2 * plan.count * plan.rows * LANES * 2 * LANES, 4 << 20),
        name="unpack_second",
    )(came, before, old, expand, *blocks)


def permutes(blocks, count):
    outs = [blocks[0]]
    for s in range(1, count):
        outs.append(lax.ppermute(blocks[s], "fourier", [(k, (k + s) % count) for k in range(count)]))
    return outs


def all_at_once(blocks):
    return lax.all_to_all(blocks, "fourier", split_axis=0, concat_axis=0, tiled=True)


def rim_exchange(low, up):
    ends = lax.axis_size("elem") - 1
    below = lax.ppermute(up, "elem", [(i, i + 1) for i in range(ends)])
    above = lax.ppermute(low, "elem", [(i + 1, i) for i in range(ends)])
    return below, above


def after(x, other):
    return lax.optimization_barrier((x, other))[0]


def chunked(plan, velocity, metric, mass_weights):
    count = plan.count
    here = lax.axis_index("fourier").astype(jnp.int32)
    steps = jnp.arange(count, dtype=jnp.int32)
    to, came = (here + steps) % count, (here - steps + count) % count
    forward, forward_left, back, back_left = (jnp.asarray(t) for t in plan.tables())
    slopes = jnp.asarray(plan.slopes())
    join, rims, expand = (jnp.asarray(t) for t in plan.assembly())
    local = jnp.concatenate([metric, mass_weights[None], jnp.zeros((3, plan.nodes), F32)], axis=0)
    tables = (forward, forward_left, slopes, join)
    back_tables = (back, back_left, rims)
    factors = []
    for q in range(CHUNKS):
        start = (here + q * count) * plan.width
        cut = lax.dynamic_slice_in_dim(local, start, plan.width, 1)
        factors.append(jnp.pad(cut, ((0, 0), (0, LANES - plan.width))))

    sent = pack_first(plan, to, velocity)
    spread = permutes(sent, count)
    second = pack_second(plan, after(to, sent[1]), velocity)
    second = all_at_once(after(second, spread))
    field, low, up = synth(plan, "synth_first", came, spread, tables, factors[0])
    below, above = rim_exchange(low, up)
    back_first = analyse(plan, "analyse_first", True, to, field, below, above, back_tables)
    back_first = all_at_once(after(back_first, second))
    field, low, up = synth(plan, "synth_second", came, second, tables, factors[1])
    below, above = rim_exchange(low, up)
    back_second = analyse(plan, "analyse_second", False, to, field, below, above, back_tables)
    returned = permutes(back_second, count)
    half = unpack_first(plan, to, back_first, expand)
    return unpack_second(plan, came, back_first, half, returned, expand)


def add_shifted(field, source, reach, side):
    count = field.shape[-1]
    node = np.arange(count)
    keep = side(node) & (node + reach >= 0) & (node + reach < count)
    pads = [(0, 0)] * (field.ndim - 1)
    if reach > 0:
        moved = jnp.pad(source[..., reach:], pads + [(0, reach)])
    else:
        moved = jnp.pad(source[..., :reach], pads + [(-reach, 0)])
    return field + jnp.where(jnp.asarray(keep), moved, 0.0)


def plain(plan, velocity, metric, mass_weights):
    count, square = plan.count, NP * NP
    synthesis, spanwise, analysis = (jnp.asarray(t, F32) for t in fourier_tables(plan.planes))
    slopes = gll_diff()
    group = plan.elements // count
    eye_elem, eye_side = np.eye(group), np.eye(NP)
    xi_matrix = jnp.asarray(np.kron(eye_elem, np.kron(eye_side, slopes.T)), F32)
    eta_matrix = jnp.asarray(np.kron(eye_elem, np.kron(slopes.T, eye_side)), F32)
    spread = lax.all_to_all(velocity, "fourier", split_axis=2, concat_axis=1, tiled=True)
    offset = lax.axis_index("fourier") * group * square
    factors = lax.dynamic_slice_in_dim(metric, offset, group * square, 1)
    weights = lax.dynamic_slice_in_dim(mass_weights, offset, group * square, 0)
    values = jnp.einsum("cmn,mz->czn", spread, synthesis, precision=HIGH)
    along_z = jnp.einsum("cmn,mz->czn", spread, spanwise, precision=HIGH)
    along_xi = jnp.einsum("czk,kn->czn", values, xi_matrix, precision=HIGH)
    along_eta = jnp.einsum("czk,kn->czn", values, eta_matrix, precision=HIGH)
    grad_x = factors[0] * along_xi + factors[2] * along_eta
    grad_y = factors[1] * along_xi + factors[3] * along_eta
    weighted = weights * (values[0] * grad_x + values[1] * grad_y + values[2] * along_z)
    coeffs = jnp.einsum("czn,mz->cmn", weighted, analysis, precision=HIGH)
    coeffs = lax.all_to_all(coeffs, "fourier", split_axis=1, concat_axis=2, tiled=True)
    last = NP - 1
    reach = square - last
    joined = add_shifted(coeffs, coeffs, reach, lambda n: n % NP == last)
    joined = add_shifted(joined, coeffs, -reach, lambda n: n % NP == 0)
    below, above = rim_exchange(joined, joined)
    result = add_shifted(joined, below, last * NP, lambda n: n % square < NP)
    return add_shifted(result, above, -last * NP, lambda n: n % square >= last * NP)


def shards(velocity, metric, mass_weights):
    plan = Plan(lax.axis_size("fourier"), velocity.shape[1], velocity.shape[2])
    step = chunked if plan.fits else plain
    return step(plan, velocity, metric, mass_weights)


def solution(mesh):
    in_specs = (P(None, "fourier", "elem"), P(None, "elem"), P("elem"))
    out_specs = P(None, "fourier", "elem")
    return jax.shard_map(shards, mesh=mesh, in_specs=in_specs, out_specs=out_specs, check_vma=False)
```

```python
import functools

import jax
import jax.numpy as jnp
import ml_dtypes
import numpy as np
from jax import lax
from jax.experimental import pallas as pl
from jax.experimental.pallas import tpu as pltpu
from jax.sharding import PartitionSpec as P

NP = 9
HIGH = lax.Precision.HIGHEST
BF = jnp.bfloat16
F32 = jnp.float32
LANES = 256
CHUNKS = 2
VMEM_LIMIT = 40 << 20


def gll_diff():
    half = [0.3631174638261782, 0.6771862795107377, 0.8997579954114602, 1.0]
    nodes = np.array([-v for v in half[::-1]] + [0.0] + half)
    points = nodes.shape[0]
    gaps = nodes[:, None] - nodes[None, :] + np.eye(points)
    bary = 1.0 / np.prod(gaps, axis=1)
    matrix = bary[None, :] / bary[:, None] / gaps
    matrix[np.arange(points), np.arange(points)] = 0.0
    matrix[np.arange(points), np.arange(points)] = -matrix.sum(axis=1)
    return matrix


def fourier_tables(planes):
    index = np.arange(planes)
    wave = (index + 1) // 2
    angles = 2.0 * np.pi * ((wave[:, None] * index[None, :]) % planes) / planes
    cosine_rows = ((index % 2 == 1) | (index == 0))[:, None]
    synthesis = np.where(cosine_rows, np.cos(angles), np.sin(angles))
    rate = wave * (8.0 / planes)
    rate[planes - 1] = 0.0
    spanwise = np.where(cosine_rows, -rate[:, None] * np.sin(angles), rate[:, None] * np.cos(angles))
    scale = np.where((index == 0) | (index == planes - 1), 1.0, 2.0) / planes
    analysis = synthesis * scale[:, None]
    return synthesis, spanwise, analysis


def halves(table):
    table = np.asarray(table, np.float32)
    high = table.astype(ml_dtypes.bfloat16)
    low = (table - high.astype(np.float32)).astype(ml_dtypes.bfloat16)
    return high, low


class Plan:
    def __init__(self, count, modes, nodes):
        self.count, self.modes, self.nodes = count, modes, nodes
        self.planes = count * modes
        self.elements = nodes // (NP * NP)
        self.main = modes // 16 * 16
        self.left = modes - self.main
        self.per_piece = self.elements // (count * CHUNKS)
        self.width = self.per_piece * NP * NP
        self.columns = self.per_piece * (NP - 1) + 1
        self.rows = 3 * self.main + 8
        self.pieces = CHUNKS * count
        self.joined = self.columns * NP
        self.stride = 14 * 128
        self.seam = -(-(count * self.width - self.width + NP * NP) // self.stride) * self.stride
        self.fits = (
            self.main > 0
            and 3 * self.left <= 8
            and self.elements % (count * CHUNKS) == 0
            and self.per_piece > 0
            and 128 < self.joined <= self.width <= LANES
            and self.seam <= count * self.width - NP * NP
            and self.columns <= 32
            and self.planes % 16 == 0
        )

    def lane(self, a, column):
        if column == 0:
            return a
        if column == self.columns - 1:
            return NP + a
        return 2 * NP + a * (self.columns - 2) + column - 1

    def tables(self):
        synthesis, spanwise, analysis = fourier_tables(self.planes)
        source = np.arange(self.count)
        main = (source[:, None] * self.modes + np.arange(self.main)[None, :]).reshape(-1)
        both = []
        for table in (synthesis, spanwise):
            high, low = halves(table.T[:, main])
            both.append(np.concatenate([high, high, low], axis=1))
        forward = np.stack(both)
        forward_left = np.zeros((3, 2, self.planes, 3 * 8 * self.count), ml_dtypes.bfloat16)
        back_left = np.zeros((3, 8 * self.count, 3 * self.planes), ml_dtypes.bfloat16)
        for c in range(3):
            for kind, table in enumerate((synthesis, spanwise)):
                wide = np.zeros((self.planes, 8 * self.count))
                for s in range(self.count):
                    for r in range(self.left):
                        wide[:, 8 * s + self.left * c + r] = table[s * self.modes + self.main + r]
                high, low = halves(wide)
                forward_left[c, kind] = np.concatenate([high, high, low], axis=1)
            tall = np.zeros((8 * self.count, self.planes))
            for s in range(self.count):
                for r in range(self.left):
                    tall[8 * s + self.left * c + r] = analysis[s * self.modes + self.main + r]
            high, low = halves(tall)
            back_left[c] = np.concatenate([high, high, low], axis=1)
        high, low = halves(analysis[main])
        back = np.concatenate([high, high, low], axis=1)
        return forward, forward_left, back, back_left

    def slopes(self):
        slopes = gll_diff()
        eye_elem, eye_side = np.eye(self.per_piece), np.eye(NP)
        wide = np.zeros((LANES, 2 * LANES))
        wide[: self.width, : self.width] = np.kron(eye_elem, np.kron(eye_side, slopes.T))
        wide[: self.width, LANES : LANES + self.width] = np.kron(eye_elem, np.kron(slopes.T, eye_side))
        high, low = halves(wide)
        return np.concatenate([high, high, low], axis=0)

    def assembly(self):
        join = np.zeros((3, LANES, 2 * LANES))
        rims = np.zeros((3, LANES, LANES))
        expand = np.zeros((LANES, LANES))
        for e in range(self.per_piece):
            for a in range(NP):
                for b in range(NP):
                    node, column = (e * NP + a) * NP + b, e * (NP - 1) + b
                    lane = self.lane(a, column)
                    expand[lane, node] = 1.0
                    for c in range(3):
                        join[c, node, lane] = 1.0
                        if a == 0:
                            join[c, node, LANES + 32 * c + column] = 1.0
                        if a == NP - 1:
                            join[c, node, LANES + 128 + 32 * c + column] = 1.0
        for c in range(3):
            for column in range(self.columns):
                rims[c, 32 * c + column, self.lane(0, column)] = 1.0
                rims[c, 128 + 32 * c + column, self.lane(NP - 1, column)] = 1.0
        kind = ml_dtypes.bfloat16
        join, rims, expand = join.astype(kind), rims.astype(kind), expand.astype(kind)
        return (
            np.concatenate([join, join], axis=1),
            np.concatenate([rims, rims], axis=1),
            np.concatenate([expand, expand], axis=0),
        )


def split(x):
    high = x.astype(BF)
    low = (x - high.astype(F32)).astype(BF)
    return high, low


def dot(a, b):
    return jnp.dot(a, b, preferred_element_type=F32)


def lane_ids():
    return lax.broadcasted_iota(jnp.int32, (8, 128), 1)


def put_rest(block, rest, rows, wide):
    lanes = lane_ids()
    count = -(-(rows // 8) * wide // 128)
    tiles = [None] * (count + 1)
    for t in range(rows // 8):
        tile, shift = t * wide // 128, t * wide % 128
        x = jnp.where(lanes < wide, rest[8 * t : 8 * t + 8, :], 0.0)
        if shift:
            x = pltpu.roll(x, shift, 1)
        parts = [(tile, jnp.where(lanes >= shift, x, 0.0) if shift else x)]
        if shift + wide > 128:
            parts.append((tile + 1, jnp.where(lanes < shift, x, 0.0)))
        for g, part in parts:
            tiles[g] = part if tiles[g] is None else tiles[g] + part
    for g in range(count):
        block[rows + 8 * g : rows + 8 * g + 8, :] = tiles[g]


def get_rest(block, t, rows, wide):
    lanes = lane_ids()
    tile, shift = t * wide // 128, t * wide % 128
    at = rows + 8 * tile
    x = block[at : at + 8, :]
    if shift + wide > 128:
        x = jnp.where(lanes >= shift, x, block[at + 8 : at + 16, :])
    return pltpu.roll(x, 128 - shift, 1) if shift else x


def wire_rows(rows, wide):
    return rows + 8 * (-(-(rows // 8) * wide // 128))


def by_step(steps, outs, buf):
    for s, out in enumerate(outs):
        out[...] = buf[steps[s]]


def pack_part(plan, piece, c, v_ref, block, rest):
    start = piece * plan.width
    base, shift = start // 128 * 128, start % 128
    wide = LANES + 128
    rows = slice(plan.main * c, plan.main * (c + 1))
    x = v_ref[c, : plan.main, base : base + wide]
    x = pltpu.roll(x, wide - shift, 1) if shift else x
    block[rows, :] = x[:, :128]
    rest[rows, :] = x[:, 128:LANES]


def pack_tail(plan, piece, v_ref, block, rest):
    start = piece * plan.width
    base, shift = start // 128 * 128, start % 128
    wide = LANES + 128
    tails = [v_ref[c, plan.main : plan.modes, base : base + wide] for c in range(3) if plan.left]
    tails.append(jnp.zeros((8 - 3 * plan.left, wide), F32))
    x = jnp.concatenate(tails, axis=0)
    x = pltpu.roll(x, wide - shift, 1) if shift else x
    block[3 * plan.main : plan.rows, :] = x[:, :128]
    rest[3 * plan.main : plan.rows, :] = x[:, 128:LANES]
    put_rest(block, rest, plan.rows, plan.width - 128)


def pack_first_kernel(plan, to_ref, v_hbm, *refs):
    outs, (held, buf, rest, sems) = refs[:-4], refs[-4:]
    reach = held.shape[2]
    copies = [
        pltpu.make_async_copy(v_hbm.at[c, :, pl.ds(0, reach)], held.at[c], sems.at[c]) for c in range(3)
    ]
    for copy in copies:
        copy.start()
    for c in range(3):
        copies[c].wait()
        for j in range(plan.count):
            pack_part(plan, j, c, held, buf.at[j], rest.at[j])
    for j in range(plan.count):
        pack_tail(plan, j, held, buf.at[j], rest.at[j])
    by_step(to_ref, outs, buf)


def pack_second_kernel(plan, gate_ref, v_ref, out_ref, rest):
    for j in range(plan.count):
        for c in range(3):
            pack_part(plan, plan.count + j, c, v_ref, out_ref.at[j], rest)
        pack_tail(plan, plan.count + j, v_ref, out_ref.at[j], rest)


def synth_kernel(plan, joined, from_ref, *refs):
    count, main = plan.count, plan.main
    blocks, refs = (refs[:1], refs[1:]) if joined else (refs[:count], refs[count:])
    t_ref, tl_ref, d_ref, join_ref, f_ref, w_ref, low_ref, up_ref, v3, raw, l3, u, dz = refs
    deep = main * count
    wide = plan.width - 128
    for s in range(count):
        source, block = (s, blocks[0].at[s]) if joined else (from_ref[s], blocks[s])
        at = source * main
        for c in range(3):
            rest = [get_rest(block, main // 8 * c + i, plan.rows, wide) for i in range(main // 8)]
            x = jnp.concatenate([block[main * c : main * (c + 1), :], jnp.concatenate(rest, axis=0)], axis=1)
            high, low = split(x)
            for i, part in enumerate((high, low, high)):
                where = i * deep + at
                v3[c, pl.ds(where if joined else pl.multiple_of(where, 16), main), :] = part
        rest = get_rest(block, 3 * main // 8, plan.rows, wide)
        where = source * 8
        x = jnp.concatenate([block[3 * main : plan.rows, :], rest], axis=1)
        raw[pl.ds(where if joined else pl.multiple_of(where, 8), 8), :] = x
    high, low = split(raw[...])
    l3[...] = jnp.concatenate([high, low, high], axis=0)

    @pl.loop(0, 3)
    def _(c):
        u[c] = dot(t_ref[0], v3[c]) + dot(tl_ref[c, 0], l3[...])
        dz[c] = dot(t_ref[1], v3[c]) + dot(tl_ref[c, 1], l3[...])

    low_ref[...] = jnp.zeros_like(low_ref)
    up_ref[...] = jnp.zeros_like(up_ref)

    @pl.loop(0, 3)
    def _(c):
        high, low = split(u[c])
        slope = dot(jnp.concatenate([high, low, high], axis=1), d_ref[...])
        along_xi, along_eta = slope[:, :LANES], slope[:, LANES:]
        grad_x = f_ref[0:1, :] * along_xi + f_ref[2:3, :] * along_eta
        grad_y = f_ref[1:2, :] * along_xi + f_ref[3:4, :] * along_eta
        weighted = f_ref[4:5, :] * (u[0] * grad_x + u[1] * grad_y + u[2] * dz[c])
        high, low = split(weighted)
        joined = dot(jnp.concatenate([high, low], axis=1), join_ref[c])
        w_ref[c] = joined[:, :LANES]
        low_ref[...] += joined[:, LANES : LANES + 128]
        up_ref[...] += joined[:, LANES + 128 :]


def analyse_kernel(plan, joined, to_ref, w_ref, below_ref, above_ref, a_ref, al_ref, rims_ref, *refs):
    outs, (w3, tail, rest) = (refs[:1], refs[1:]) if joined else (refs[: plan.count], refs[plan.count + 1 :])
    buf = outs[0] if joined else refs[plan.count]
    count, main = plan.count, plan.main
    high, low = split(jnp.concatenate([below_ref[...], above_ref[...]], axis=1))
    rims = jnp.concatenate([high, low], axis=1)
    tail[...] = jnp.zeros_like(tail)

    @pl.loop(0, 3)
    def _(c):
        high, low = split(w_ref[c] + dot(rims, rims_ref[c]))
        w3[...] = jnp.concatenate([high, low, high], axis=0)
        coeffs = dot(a_ref[...], w3[...])
        rows = pl.ds(pl.multiple_of(c * main, main), main)
        for d in range(count):
            buf[d, rows, :] = coeffs[main * d : main * (d + 1), :128]
            rest[d, rows, :] = coeffs[main * d : main * (d + 1), 128:]
        tail[...] += dot(al_ref[c], w3[...])

    for d in range(count):
        buf[d, 3 * main : plan.rows, :] = tail[8 * d : 8 * (d + 1), :128]
        rest[d, 3 * main : plan.rows, :] = tail[8 * d : 8 * (d + 1), 128:]
        put_rest(buf.at[d], rest.at[d], plan.rows, plan.joined - 128)
    if not joined:
        by_step(to_ref, outs, buf)


def unpack_lanes(plan, held, e_ref, lhs, grown, out_ref, base):
    rows, wide = plan.rows, plan.joined - 128
    pad = -(-rows // 16) * 16
    span = out_ref.shape[2]
    lanes = lax.broadcasted_iota(jnp.int32, (1, 128), 1)
    pieces = [i for i in range(plan.pieces) if i * plan.width < base + span and (i + 1) * plan.width > base]
    for n, i in enumerate(pieces):
        x = held[i][:rows, :]
        if i - 1 in held:
            x = x + jnp.where(lanes < NP, pltpu.roll(held[i - 1][:rows, :], 128 - NP, 1), 0.0)
        if i + 1 in held:
            inside = (lanes >= NP) & (lanes < 2 * NP)
            x = x + jnp.where(inside, pltpu.roll(held[i + 1][:rows, :], NP, 1), 0.0)
        rest = jnp.concatenate([get_rest(held[i], t, rows, wide) for t in range(rows // 8)], axis=0)
        x = jnp.concatenate([x, rest], axis=1)
        if pad > rows:
            x = jnp.concatenate([x, jnp.zeros((pad - rows, LANES), F32)], axis=0)
        high, low = split(x)
        lhs[pad * n : pad * (n + 1), :] = jnp.concatenate([high, low], axis=1)
        if n % 1 == 0 or n == len(pieces) - 1:
            ready = slice(pad * (n // 1 * 1), pad * (n + 1))
            grown[ready, :] = dot(lhs[ready, :], e_ref[...])
    tiles = {}
    for n, i in enumerate(pieces):
        for half in range(2):
            start = i * plan.width + 128 * half - base
            tile, shift = start // 128, start % 128
            x = grown[pad * n : pad * n + rows, 128 * half : 128 * (half + 1)]
            x = pltpu.roll(x, shift, 1) if shift else x
            tiles[tile] = jnp.where(lanes >= shift, x, tiles[tile]) if shift and tile in tiles else x
            if shift:
                tiles[tile + 1] = x
    for tile in range(span // 128):
        x = tiles.get(tile)
        if x is None:
            continue
        at = slice(128 * tile, 128 * (tile + 1))
        for c in range(3):
            out_ref[c, : plan.main, at] = x[plan.main * c : plan.main * (c + 1), :]
            if plan.left:
                row = 3 * plan.main + plan.left * c
                out_ref[c, plan.main :, at] = x[row : row + plan.left, :]


def unpack_first_kernel(plan, gate_ref, block_ref, e_ref, out_ref, lhs, grown):
    held = {i: block_ref.at[i] for i in range(plan.count)}
    unpack_lanes(plan, held, e_ref, lhs, grown, out_ref, 0)


def unpack_second_kernel(plan, steps, from_ref, before_ref, old_ref, e_ref, *refs):
    blocks, (out_ref, buf, lhs, grown) = refs[: plan.count], refs[plan.count :]
    step = pl.program_id(0)
    held = {plan.count + j: buf.at[j] for j in range(plan.count)}
    held[plan.count - 1] = before_ref.at[0]

    @pl.when(step == 0)
    def _():
        for s in range(plan.count):
            buf[from_ref[s]] = blocks[s][...]

    for i in range(steps):

        @pl.when(step == i)
        def _():
            unpack_lanes(plan, held, e_ref, lhs, grown, out_ref, plan.seam + i * plan.stride)


def smem():
    return pl.BlockSpec(memory_space=pltpu.SMEM)


def vmem():
    return pl.BlockSpec(memory_space=pltpu.VMEM)


def hbm():
    return pl.BlockSpec(memory_space=pl.ANY)


def params():
    return pltpu.CompilerParams(vmem_limit_bytes=VMEM_LIMIT)


def cost(flops, size):
    return pl.CostEstimate(flops=int(flops), bytes_accessed=int(size), transcendentals=0)


def pack_first(plan, to, velocity):
    last = (plan.count - 1) * plan.width
    reach = last // 128 * 128 + LANES + 128
    tall = wire_rows(plan.rows, plan.width - 128)
    return pl.pallas_call(
        functools.partial(pack_first_kernel, plan),
        in_specs=[smem(), pl.BlockSpec(memory_space=pltpu.MemorySpace.HBM)],
        out_specs=[vmem()] * plan.count,
        out_shape=[jax.ShapeDtypeStruct((tall, 128), F32)] * plan.count,
        scratch_shapes=[
            pltpu.VMEM((3, plan.modes, reach), F32),
            pltpu.VMEM((plan.count, tall, 128), F32),
            pltpu.VMEM((plan.count, plan.rows, 128), F32),
            pltpu.SemaphoreType.DMA((3,)),
        ],
        compiler_params=params(),
        cost_estimate=cost(0, 8 * plan.count * tall * 128),
        name="pack_first",
    )(to, pltpu.with_memory_space_constraint(velocity, pltpu.MemorySpace.HBM))


def pack_second(plan, gate, velocity):
    span = -(-plan.nodes // 128) * 128
    tall = wire_rows(plan.rows, plan.width - 128)
    return pl.pallas_call(
        functools.partial(pack_second_kernel, plan),
        grid=(1,),
        in_specs=[smem(), pl.BlockSpec((3, plan.modes, span), lambda i: (0, 0, 0))],
        out_specs=vmem(),
        out_shape=jax.ShapeDtypeStruct((plan.count, tall, 128), F32),
        scratch_shapes=[pltpu.VMEM((plan.rows, 128), F32)],
        compiler_params=params(),
        cost_estimate=cost(0, 8 * plan.count * tall * 128),
        name="pack_second",
    )(gate, pltpu.with_memory_space_constraint(velocity, pltpu.MemorySpace.HBM))


def synth(plan, name, came, blocks, tables, factors):
    joined = not isinstance(blocks, list)
    blocks = [blocks] if joined else blocks
    deep = plan.main * plan.count
    small = 8 * plan.count
    field = jax.ShapeDtypeStruct((3, plan.planes, LANES), F32)
    rim = jax.ShapeDtypeStruct((plan.planes, 128), F32)
    return pl.pallas_call(
        functools.partial(synth_kernel, plan, joined),
        in_specs=[smem()] + [vmem()] * (len(blocks) + 5),
        out_specs=[vmem()] * 3,
        out_shape=[field, rim, rim],
        scratch_shapes=[
            pltpu.VMEM((3, 3 * deep, LANES), BF),
            pltpu.VMEM((small, LANES), F32),
            pltpu.VMEM((3 * small, LANES), BF),
            pltpu.VMEM((3, plan.planes, LANES), F32),
            pltpu.VMEM((3, plan.planes, LANES), F32),
        ],
        compiler_params=params(),
        cost_estimate=cost(3 * 2 * plan.planes * LANES * (6 * deep + 6 * LANES + 4 * LANES), 12 << 20),
        name=name,
    )(came, *blocks, *tables, factors)


def analyse(plan, name, joined, to, field, below, above, tables):
    count = plan.count
    tall = wire_rows(plan.rows, plan.joined - 128)
    if joined:
        shape, specs, extra = jax.ShapeDtypeStruct((count, tall, 128), F32), vmem(), []
    else:
        shape, specs = [jax.ShapeDtypeStruct((tall, 128), F32)] * count, [vmem()] * count
        extra = [pltpu.VMEM((count, tall, 128), F32)]
    return pl.pallas_call(
        functools.partial(analyse_kernel, plan, joined),
        in_specs=[smem()] + [vmem()] * 6,
        out_specs=specs,
        out_shape=shape,
        scratch_shapes=extra
        + [
            pltpu.VMEM((3 * plan.planes, LANES), BF),
            pltpu.VMEM((8 * count, LANES), F32),
            pltpu.VMEM((count, plan.rows, 128), F32),
        ],
        compiler_params=params(),
        cost_estimate=cost(3 * 2 * plan.planes * LANES * 3 * plan.planes, 6 << 20),
        name=name,
    )(to, field, below, above, *tables)


def unpack_scratch(plan, span):
    pieces = min(plan.pieces, -(-span // plan.width) + 1)
    pad = -(-plan.rows // 16) * 16
    return [pltpu.VMEM((pieces * pad, 2 * LANES), BF), pltpu.VMEM((pieces * pad, LANES), F32)]


def unpack_first(plan, gate, blocks, expand):
    out = jax.ShapeDtypeStruct((3, plan.modes, plan.nodes), F32)
    return pl.pallas_call(
        functools.partial(unpack_first_kernel, plan),
        grid=(1,),
        in_specs=[smem(), vmem(), vmem()],
        out_specs=pl.BlockSpec((3, plan.modes, plan.seam), lambda i: (0, 0, 0)),
        out_shape=out,
        scratch_shapes=unpack_scratch(plan, plan.seam),
        compiler_params=params(),
        cost_estimate=cost(2 * plan.count * plan.rows * LANES * 2 * LANES, 4 << 20),
        name="unpack_first",
    )(gate, blocks, expand)


def unpack_second(plan, came, before, old, blocks, expand):
    tall = blocks[0].shape[0]
    steps = -(-(plan.nodes - plan.seam) // plan.stride)
    skip = plan.seam // plan.stride
    return pl.pallas_call(
        functools.partial(unpack_second_kernel, plan, steps),
        grid=(steps,),
        in_specs=[
            smem(),
            pl.BlockSpec((1, tall, 128), lambda i: (plan.count - 1, 0, 0)),
            hbm(),
            pl.BlockSpec(expand.shape, lambda i: (0, 0)),
        ]
        + [pl.BlockSpec((tall, 128), lambda i: (0, 0))] * plan.count,
        out_specs=pl.BlockSpec((3, plan.modes, plan.stride), lambda i: (0, 0, i + skip)),
        out_shape=jax.ShapeDtypeStruct((3, plan.modes, plan.nodes), F32),
        scratch_shapes=[pltpu.VMEM((plan.count, tall, 128), F32)] + unpack_scratch(plan, plan.stride),
        input_output_aliases={2: 0},
        compiler_params=params(),
        cost_estimate=cost(2 * plan.count * plan.rows * LANES * 2 * LANES, 4 << 20),
        name="unpack_second",
    )(came, before, old, expand, *blocks)


def permutes(blocks, count):
    outs = [blocks[0]]
    for s in range(1, count):
        outs.append(lax.ppermute(blocks[s], "fourier", [(k, (k + s) % count) for k in range(count)]))
    return outs


def all_at_once(blocks):
    return lax.all_to_all(blocks, "fourier", split_axis=0, concat_axis=0, tiled=True)


def rim_exchange(low, up):
    ends = lax.axis_size("elem") - 1
    below = lax.ppermute(up, "elem", [(i, i + 1) for i in range(ends)])
    above = lax.ppermute(low, "elem", [(i + 1, i) for i in range(ends)])
    return below, above


def after(x, other):
    return lax.optimization_barrier((x, other))[0]


def chunked(plan, velocity, metric, mass_weights):
    count = plan.count
    here = lax.axis_index("fourier").astype(jnp.int32)
    steps = jnp.arange(count, dtype=jnp.int32)
    to, came = (here + steps) % count, (here - steps + count) % count
    forward, forward_left, back, back_left = (jnp.asarray(t) for t in plan.tables())
    slopes = jnp.asarray(plan.slopes())
    join, rims, expand = (jnp.asarray(t) for t in plan.assembly())
    local = jnp.concatenate([metric, mass_weights[None], jnp.zeros((3, plan.nodes), F32)], axis=0)
    tables = (forward, forward_left, slopes, join)
    back_tables = (back, back_left, rims)
    factors = []
    for q in range(CHUNKS):
        start = (here + q * count) * plan.width
        cut = lax.dynamic_slice_in_dim(local, start, plan.width, 1)
        factors.append(jnp.pad(cut, ((0, 0), (0, LANES - plan.width))))

    sent = pack_first(plan, to, velocity)
    spread = permutes(sent, count)
    second = pack_second(plan, after(to, sent[1]), velocity)
    second = all_at_once(after(second, spread))
    field, low, up = synth(plan, "synth_first", came, spread, tables, factors[0])
    below, above = rim_exchange(low, up)
    back_first = analyse(plan, "analyse_first", True, to, field, below, above, back_tables)
    back_first = all_at_once(after(back_first, second))
    field, low, up = synth(plan, "synth_second", came, second, tables, factors[1])
    below, above = rim_exchange(low, up)
    back_second = analyse(plan, "analyse_second", False, to, field, below, above, back_tables)
    returned = permutes(back_second, count)
    half = unpack_first(plan, to, back_first, expand)
    return unpack_second(plan, came, back_first, half, returned, expand)


def add_shifted(field, source, reach, side):
    count = field.shape[-1]
    node = np.arange(count)
    keep = side(node) & (node + reach >= 0) & (node + reach < count)
    pads = [(0, 0)] * (field.ndim - 1)
    if reach > 0:
        moved = jnp.pad(source[..., reach:], pads + [(0, reach)])
    else:
        moved = jnp.pad(source[..., :reach], pads + [(-reach, 0)])
    return field + jnp.where(jnp.asarray(keep), moved, 0.0)


def plain(plan, velocity, metric, mass_weights):
    count, square = plan.count, NP * NP
    synthesis, spanwise, analysis = (jnp.asarray(t, F32) for t in fourier_tables(plan.planes))
    slopes = gll_diff()
    group = plan.elements // count
    eye_elem, eye_side = np.eye(group), np.eye(NP)
    xi_matrix = jnp.asarray(np.kron(eye_elem, np.kron(eye_side, slopes.T)), F32)
    eta_matrix = jnp.asarray(np.kron(eye_elem, np.kron(slopes.T, eye_side)), F32)
    spread = lax.all_to_all(velocity, "fourier", split_axis=2, concat_axis=1, tiled=True)
    offset = lax.axis_index("fourier") * group * square
    factors = lax.dynamic_slice_in_dim(metric, offset, group * square, 1)
    weights = lax.dynamic_slice_in_dim(mass_weights, offset, group * square, 0)
    values = jnp.einsum("cmn,mz->czn", spread, synthesis, precision=HIGH)
    along_z = jnp.einsum("cmn,mz->czn", spread, spanwise, precision=HIGH)
    along_xi = jnp.einsum("czk,kn->czn", values, xi_matrix, precision=HIGH)
    along_eta = jnp.einsum("czk,kn->czn", values, eta_matrix, precision=HIGH)
    grad_x = factors[0] * along_xi + factors[2] * along_eta
    grad_y = factors[1] * along_xi + factors[3] * along_eta
    weighted = weights * (values[0] * grad_x + values[1] * grad_y + values[2] * along_z)
    coeffs = jnp.einsum("czn,mz->cmn", weighted, analysis, precision=HIGH)
    coeffs = lax.all_to_all(coeffs, "fourier", split_axis=1, concat_axis=2, tiled=True)
    last = NP - 1
    reach = square - last
    joined = add_shifted(coeffs, coeffs, reach, lambda n: n % NP == last)
    joined = add_shifted(joined, coeffs, -reach, lambda n: n % NP == 0)
    below, above = rim_exchange(joined, joined)
    result = add_shifted(joined, below, last * NP, lambda n: n % square < NP)
    return add_shifted(result, above, -last * NP, lambda n: n % square >= last * NP)


def shards(velocity, metric, mass_weights):
    plan = Plan(lax.axis_size("fourier"), velocity.shape[1], velocity.shape[2])
    step = chunked if plan.fits else plain
    return step(plan, velocity, metric, mass_weights)


def solution(mesh):
    in_specs = (P(None, "fourier", "elem"), P(None, "elem"), P("elem"))
    out_specs = P(None, "fourier", "elem")
    return jax.shard_map(shards, mesh=mesh, in_specs=in_specs, out_specs=out_specs, check_vma=False)
```

```python
import functools

import jax
import jax.numpy as jnp
import ml_dtypes
import numpy as np
from jax import lax
from jax.experimental import pallas as pl
from jax.experimental.pallas import tpu as pltpu
from jax.sharding import PartitionSpec as P

NP = 9
HIGH = lax.Precision.HIGHEST
BF = jnp.bfloat16
F32 = jnp.float32
LANES = 256
CHUNKS = 2
VMEM_LIMIT = 40 << 20


def gll_diff():
    half = [0.3631174638261782, 0.6771862795107377, 0.8997579954114602, 1.0]
    nodes = np.array([-v for v in half[::-1]] + [0.0] + half)
    points = nodes.shape[0]
    gaps = nodes[:, None] - nodes[None, :] + np.eye(points)
    bary = 1.0 / np.prod(gaps, axis=1)
    matrix = bary[None, :] / bary[:, None] / gaps
    matrix[np.arange(points), np.arange(points)] = 0.0
    matrix[np.arange(points), np.arange(points)] = -matrix.sum(axis=1)
    return matrix


def fourier_tables(planes):
    index = np.arange(planes)
    wave = (index + 1) // 2
    angles = 2.0 * np.pi * ((wave[:, None] * index[None, :]) % planes) / planes
    cosine_rows = ((index % 2 == 1) | (index == 0))[:, None]
    synthesis = np.where(cosine_rows, np.cos(angles), np.sin(angles))
    rate = wave * (8.0 / planes)
    rate[planes - 1] = 0.0
    spanwise = np.where(cosine_rows, -rate[:, None] * np.sin(angles), rate[:, None] * np.cos(angles))
    scale = np.where((index == 0) | (index == planes - 1), 1.0, 2.0) / planes
    analysis = synthesis * scale[:, None]
    return synthesis, spanwise, analysis


def halves(table):
    table = np.asarray(table, np.float32)
    high = table.astype(ml_dtypes.bfloat16)
    low = (table - high.astype(np.float32)).astype(ml_dtypes.bfloat16)
    return high, low


class Plan:
    def __init__(self, count, modes, nodes):
        self.count, self.modes, self.nodes = count, modes, nodes
        self.planes = count * modes
        self.elements = nodes // (NP * NP)
        self.main = modes // 16 * 16
        self.left = modes - self.main
        self.per_piece = self.elements // (count * CHUNKS)
        self.width = self.per_piece * NP * NP
        self.columns = self.per_piece * (NP - 1) + 1
        self.rows = 3 * self.main + 8
        self.pieces = CHUNKS * count
        self.joined = self.columns * NP
        self.stride = 14 * 128
        self.seam = -(-(count * self.width - self.width + NP * NP) // self.stride) * self.stride
        self.fits = (
            self.main > 0
            and 3 * self.left <= 8
            and self.elements % (count * CHUNKS) == 0
            and self.per_piece > 0
            and 128 < self.joined <= self.width <= LANES
            and self.seam <= count * self.width - NP * NP
            and self.columns <= 32
            and self.planes % 16 == 0
        )

    def lane(self, a, column):
        if column == 0:
            return a
        if column == self.columns - 1:
            return NP + a
        return 2 * NP + a * (self.columns - 2) + column - 1

    def tables(self):
        synthesis, spanwise, analysis = fourier_tables(self.planes)
        source = np.arange(self.count)
        main = (source[:, None] * self.modes + np.arange(self.main)[None, :]).reshape(-1)
        both = []
        for table in (synthesis, spanwise):
            high, low = halves(table.T[:, main])
            both.append(np.concatenate([high, high, low], axis=1))
        forward = np.stack(both)
        forward_left = np.zeros((3, 2, self.planes, 3 * 8 * self.count), ml_dtypes.bfloat16)
        back_left = np.zeros((3, 8 * self.count, 3 * self.planes), ml_dtypes.bfloat16)
        for c in range(3):
            for kind, table in enumerate((synthesis, spanwise)):
                wide = np.zeros((self.planes, 8 * self.count))
                for s in range(self.count):
                    for r in range(self.left):
                        wide[:, 8 * s + self.left * c + r] = table[s * self.modes + self.main + r]
                high, low = halves(wide)
                forward_left[c, kind] = np.concatenate([high, high, low], axis=1)
            tall = np.zeros((8 * self.count, self.planes))
            for s in range(self.count):
                for r in range(self.left):
                    tall[8 * s + self.left * c + r] = analysis[s * self.modes + self.main + r]
            high, low = halves(tall)
            back_left[c] = np.concatenate([high, high, low], axis=1)
        high, low = halves(analysis[main])
        back = np.concatenate([high, high, low], axis=1)
        return forward, forward_left, back, back_left

    def slopes(self):
        slopes = gll_diff()
        eye_elem, eye_side = np.eye(self.per_piece), np.eye(NP)
        wide = np.zeros((LANES, 2 * LANES))
        wide[: self.width, : self.width] = np.kron(eye_elem, np.kron(eye_side, slopes.T))
        wide[: self.width, LANES : LANES + self.width] = np.kron(eye_elem, np.kron(slopes.T, eye_side))
        high, low = halves(wide)
        return np.concatenate([high, high, low], axis=0)

    def assembly(self):
        join = np.zeros((3, LANES, 2 * LANES))
        rims = np.zeros((3, LANES, LANES))
        expand = np.zeros((LANES, LANES))
        for e in range(self.per_piece):
            for a in range(NP):
                for b in range(NP):
                    node, column = (e * NP + a) * NP + b, e * (NP - 1) + b
                    lane = self.lane(a, column)
                    expand[lane, node] = 1.0
                    for c in range(3):
                        join[c, node, lane] = 1.0
                        if a == 0:
                            join[c, node, LANES + 32 * c + column] = 1.0
                        if a == NP - 1:
                            join[c, node, LANES + 128 + 32 * c + column] = 1.0
        for c in range(3):
            for column in range(self.columns):
                rims[c, 32 * c + column, self.lane(0, column)] = 1.0
                rims[c, 128 + 32 * c + column, self.lane(NP - 1, column)] = 1.0
        kind = ml_dtypes.bfloat16
        join, rims, expand = join.astype(kind), rims.astype(kind), expand.astype(kind)
        return (
            np.concatenate([join, join], axis=1),
            np.concatenate([rims, rims], axis=1),
            np.concatenate([expand, expand], axis=0),
        )


def split(x):
    high = x.astype(BF)
    low = (x - high.astype(F32)).astype(BF)
    return high, low


def dot(a, b):
    return jnp.dot(a, b, preferred_element_type=F32)


def lane_ids():
    return lax.broadcasted_iota(jnp.int32, (8, 128), 1)


def put_rest(block, rest, rows, wide):
    lanes = lane_ids()
    count = -(-(rows // 8) * wide // 128)
    tiles = [None] * (count + 1)
    for t in range(rows // 8):
        tile, shift = t * wide // 128, t * wide % 128
        x = jnp.where(lanes < wide, rest[8 * t : 8 * t + 8, :], 0.0)
        if shift:
            x = pltpu.roll(x, shift, 1)
        parts = [(tile, jnp.where(lanes >= shift, x, 0.0) if shift else x)]
        if shift + wide > 128:
            parts.append((tile + 1, jnp.where(lanes < shift, x, 0.0)))
        for g, part in parts:
            tiles[g] = part if tiles[g] is None else tiles[g] + part
    for g in range(count):
        block[rows + 8 * g : rows + 8 * g + 8, :] = tiles[g]


def get_rest(block, t, rows, wide):
    lanes = lane_ids()
    tile, shift = t * wide // 128, t * wide % 128
    at = rows + 8 * tile
    x = block[at : at + 8, :]
    if shift + wide > 128:
        x = jnp.where(lanes >= shift, x, block[at + 8 : at + 16, :])
    return pltpu.roll(x, 128 - shift, 1) if shift else x


def wire_rows(rows, wide):
    return rows + 8 * (-(-(rows // 8) * wide // 128))


def by_step(steps, outs, buf):
    for s, out in enumerate(outs):
        out[...] = buf[steps[s]]


def pack_part(plan, piece, c, v_ref, block, rest):
    start = piece * plan.width
    base, shift = start // 128 * 128, start % 128
    wide = LANES + 128
    rows = slice(plan.main * c, plan.main * (c + 1))
    x = v_ref[c, : plan.main, base : base + wide]
    x = pltpu.roll(x, wide - shift, 1) if shift else x
    block[rows, :] = x[:, :128]
    rest[rows, :] = x[:, 128:LANES]


def pack_tail(plan, piece, v_ref, block, rest):
    start = piece * plan.width
    base, shift = start // 128 * 128, start % 128
    wide = LANES + 128
    tails = [v_ref[c, plan.main : plan.modes, base : base + wide] for c in range(3) if plan.left]
    tails.append(jnp.zeros((8 - 3 * plan.left, wide), F32))
    x = jnp.concatenate(tails, axis=0)
    x = pltpu.roll(x, wide - shift, 1) if shift else x
    block[3 * plan.main : plan.rows, :] = x[:, :128]
    rest[3 * plan.main : plan.rows, :] = x[:, 128:LANES]
    put_rest(block, rest, plan.rows, plan.width - 128)


def pack_first_kernel(plan, to_ref, v_hbm, *refs):
    outs, (held, buf, rest, sems) = refs[:-4], refs[-4:]
    reach = held.shape[2]
    copies = [
        pltpu.make_async_copy(v_hbm.at[c, :, pl.ds(0, reach)], held.at[c], sems.at[c]) for c in range(3)
    ]
    for copy in copies:
        copy.start()
    for c in range(3):
        copies[c].wait()
        for j in range(plan.count):
            pack_part(plan, j, c, held, buf.at[j], rest.at[j])
    for j in range(plan.count):
        pack_tail(plan, j, held, buf.at[j], rest.at[j])
    by_step(to_ref, outs, buf)


def pack_second_kernel(plan, gate_ref, v_ref, out_ref, rest):
    for j in range(plan.count):
        for c in range(3):
            pack_part(plan, plan.count + j, c, v_ref, out_ref.at[j], rest)
        pack_tail(plan, plan.count + j, v_ref, out_ref.at[j], rest)


def synth_kernel(plan, joined, from_ref, *refs):
    count, main = plan.count, plan.main
    blocks, refs = (refs[:1], refs[1:]) if joined else (refs[:count], refs[count:])
    t_ref, tl_ref, d_ref, join_ref, f_ref, w_ref, low_ref, up_ref, v3, raw, l3, u, dz = refs
    deep = main * count
    wide = plan.width - 128
    for s in range(count):
        source, block = (s, blocks[0].at[s]) if joined else (from_ref[s], blocks[s])
        at = source * main
        for c in range(3):
            rest = [get_rest(block, main // 8 * c + i, plan.rows, wide) for i in range(main // 8)]
            x = jnp.concatenate([block[main * c : main * (c + 1), :], jnp.concatenate(rest, axis=0)], axis=1)
            high, low = split(x)
            for i, part in enumerate((high, low, high)):
                where = i * deep + at
                v3[c, pl.ds(where if joined else pl.multiple_of(where, 16), main), :] = part
        rest = get_rest(block, 3 * main // 8, plan.rows, wide)
        where = source * 8
        x = jnp.concatenate([block[3 * main : plan.rows, :], rest], axis=1)
        raw[pl.ds(where if joined else pl.multiple_of(where, 8), 8), :] = x
    high, low = split(raw[...])
    l3[...] = jnp.concatenate([high, low, high], axis=0)

    @pl.loop(0, 3)
    def _(c):
        u[c] = dot(t_ref[0], v3[c]) + dot(tl_ref[c, 0], l3[...])
        dz[c] = dot(t_ref[1], v3[c]) + dot(tl_ref[c, 1], l3[...])

    low_ref[...] = jnp.zeros_like(low_ref)
    up_ref[...] = jnp.zeros_like(up_ref)

    @pl.loop(0, 3)
    def _(c):
        high, low = split(u[c])
        slope = dot(jnp.concatenate([high, low, high], axis=1), d_ref[...])
        along_xi, along_eta = slope[:, :LANES], slope[:, LANES:]
        grad_x = f_ref[0:1, :] * along_xi + f_ref[2:3, :] * along_eta
        grad_y = f_ref[1:2, :] * along_xi + f_ref[3:4, :] * along_eta
        weighted = f_ref[4:5, :] * (u[0] * grad_x + u[1] * grad_y + u[2] * dz[c])
        high, low = split(weighted)
        joined = dot(jnp.concatenate([high, low], axis=1), join_ref[c])
        w_ref[c] = joined[:, :LANES]
        low_ref[...] += joined[:, LANES : LANES + 128]
        up_ref[...] += joined[:, LANES + 128 :]


def analyse_kernel(plan, joined, to_ref, w_ref, below_ref, above_ref, a_ref, al_ref, rims_ref, *refs):
    outs, (w3, tail, rest) = (refs[:1], refs[1:]) if joined else (refs[: plan.count], refs[plan.count + 1 :])
    buf = outs[0] if joined else refs[plan.count]
    count, main = plan.count, plan.main
    high, low = split(jnp.concatenate([below_ref[...], above_ref[...]], axis=1))
    rims = jnp.concatenate([high, low], axis=1)
    tail[...] = jnp.zeros_like(tail)

    @pl.loop(0, 3)
    def _(c):
        high, low = split(w_ref[c] + dot(rims, rims_ref[c]))
        w3[...] = jnp.concatenate([high, low, high], axis=0)
        coeffs = dot(a_ref[...], w3[...])
        rows = pl.ds(pl.multiple_of(c * main, main), main)
        for d in range(count):
            buf[d, rows, :] = coeffs[main * d : main * (d + 1), :128]
            rest[d, rows, :] = coeffs[main * d : main * (d + 1), 128:]
        tail[...] += dot(al_ref[c], w3[...])

    for d in range(count):
        buf[d, 3 * main : plan.rows, :] = tail[8 * d : 8 * (d + 1), :128]
        rest[d, 3 * main : plan.rows, :] = tail[8 * d : 8 * (d + 1), 128:]
        put_rest(buf.at[d], rest.at[d], plan.rows, plan.joined - 128)
    if not joined:
        by_step(to_ref, outs, buf)


def unpack_lanes(plan, held, e_ref, lhs, grown, out_ref, base):
    rows, wide = plan.rows, plan.joined - 128
    pad = -(-rows // 16) * 16
    span = out_ref.shape[2]
    lanes = lax.broadcasted_iota(jnp.int32, (1, 128), 1)
    pieces = [i for i in range(plan.pieces) if i * plan.width < base + span and (i + 1) * plan.width > base]
    for n, i in enumerate(pieces):
        x = held[i][:rows, :]
        if i - 1 in held:
            x = x + jnp.where(lanes < NP, pltpu.roll(held[i - 1][:rows, :], 128 - NP, 1), 0.0)
        if i + 1 in held:
            inside = (lanes >= NP) & (lanes < 2 * NP)
            x = x + jnp.where(inside, pltpu.roll(held[i + 1][:rows, :], NP, 1), 0.0)
        rest = jnp.concatenate([get_rest(held[i], t, rows, wide) for t in range(rows // 8)], axis=0)
        x = jnp.concatenate([x, rest], axis=1)
        if pad > rows:
            x = jnp.concatenate([x, jnp.zeros((pad - rows, LANES), F32)], axis=0)
        high, low = split(x)
        lhs[pad * n : pad * (n + 1), :] = jnp.concatenate([high, low], axis=1)
        if n % 1 == 0 or n == len(pieces) - 1:
            ready = slice(pad * (n // 1 * 1), pad * (n + 1))
            grown[ready, :] = dot(lhs[ready, :], e_ref[...])
    tiles = {}
    for n, i in enumerate(pieces):
        for half in range(2):
            start = i * plan.width + 128 * half - base
            tile, shift = start // 128, start % 128
            x = grown[pad * n : pad * n + rows, 128 * half : 128 * (half + 1)]
            x = pltpu.roll(x, shift, 1) if shift else x
            tiles[tile] = jnp.where(lanes >= shift, x, tiles[tile]) if shift and tile in tiles else x
            if shift:
                tiles[tile + 1] = x
    for tile in range(span // 128):
        x = tiles.get(tile)
        if x is None:
            continue
        at = slice(128 * tile, 128 * (tile + 1))
        for c in range(3):
            out_ref[c, : plan.main, at] = x[plan.main * c : plan.main * (c + 1), :]
            if plan.left:
                row = 3 * plan.main + plan.left * c
                out_ref[c, plan.main :, at] = x[row : row + plan.left, :]


def unpack_first_kernel(plan, gate_ref, block_ref, e_ref, out_ref, lhs, grown):
    held = {i: block_ref.at[i] for i in range(plan.count)}
    unpack_lanes(plan, held, e_ref, lhs, grown, out_ref, 0)


def unpack_second_kernel(plan, steps, from_ref, before_ref, old_ref, e_ref, *refs):
    blocks, (out_ref, buf, lhs, grown) = refs[: plan.count], refs[plan.count :]
    step = pl.program_id(0)
    held = {plan.count + j: buf.at[j] for j in range(plan.count)}
    held[plan.count - 1] = before_ref.at[0]

    @pl.when(step == 0)
    def _():
        for s in range(plan.count):
            buf[from_ref[s]] = blocks[s][...]

    for i in range(steps):

        @pl.when(step == i)
        def _():
            unpack_lanes(plan, held, e_ref, lhs, grown, out_ref, plan.seam + i * plan.stride)


def smem():
    return pl.BlockSpec(memory_space=pltpu.SMEM)


def vmem():
    return pl.BlockSpec(memory_space=pltpu.VMEM)


def hbm():
    return pl.BlockSpec(memory_space=pl.ANY)


def params():
    return pltpu.CompilerParams(vmem_limit_bytes=VMEM_LIMIT)


def cost(flops, size):
    return pl.CostEstimate(flops=int(flops), bytes_accessed=int(size), transcendentals=0)


def pack_first(plan, to, velocity):
    last = (plan.count - 1) * plan.width
    reach = last // 128 * 128 + LANES + 128
    tall = wire_rows(plan.rows, plan.width - 128)
    return pl.pallas_call(
        functools.partial(pack_first_kernel, plan),
        in_specs=[smem(), pl.BlockSpec(memory_space=pltpu.MemorySpace.HBM)],
        out_specs=[vmem()] * plan.count,
        out_shape=[jax.ShapeDtypeStruct((tall, 128), F32)] * plan.count,
        scratch_shapes=[
            pltpu.VMEM((3, plan.modes, reach), F32),
            pltpu.VMEM((plan.count, tall, 128), F32),
            pltpu.VMEM((plan.count, plan.rows, 128), F32),
            pltpu.SemaphoreType.DMA((3,)),
        ],
        compiler_params=params(),
        cost_estimate=cost(0, 8 * plan.count * tall * 128),
        name="pack_first",
    )(to, pltpu.with_memory_space_constraint(velocity, pltpu.MemorySpace.HBM))


def pack_second(plan, gate, velocity):
    span = -(-plan.nodes // 128) * 128
    tall = wire_rows(plan.rows, plan.width - 128)
    return pl.pallas_call(
        functools.partial(pack_second_kernel, plan),
        grid=(1,),
        in_specs=[smem(), pl.BlockSpec((3, plan.modes, span), lambda i: (0, 0, 0))],
        out_specs=vmem(),
        out_shape=jax.ShapeDtypeStruct((plan.count, tall, 128), F32),
        scratch_shapes=[pltpu.VMEM((plan.rows, 128), F32)],
        compiler_params=params(),
        cost_estimate=cost(0, 8 * plan.count * tall * 128),
        name="pack_second",
    )(gate, pltpu.with_memory_space_constraint(velocity, pltpu.MemorySpace.HBM))


def synth(plan, name, came, blocks, tables, factors):
    joined = not isinstance(blocks, list)
    blocks = [blocks] if joined else blocks
    deep = plan.main * plan.count
    small = 8 * plan.count
    field = jax.ShapeDtypeStruct((3, plan.planes, LANES), F32)
    rim = jax.ShapeDtypeStruct((plan.planes, 128), F32)
    return pl.pallas_call(
        functools.partial(synth_kernel, plan, joined),
        in_specs=[smem()] + [vmem()] * (len(blocks) + 5),
        out_specs=[vmem()] * 3,
        out_shape=[field, rim, rim],
        scratch_shapes=[
            pltpu.VMEM((3, 3 * deep, LANES), BF),
            pltpu.VMEM((small, LANES), F32),
            pltpu.VMEM((3 * small, LANES), BF),
            pltpu.VMEM((3, plan.planes, LANES), F32),
            pltpu.VMEM((3, plan.planes, LANES), F32),
        ],
        compiler_params=params(),
        cost_estimate=cost(3 * 2 * plan.planes * LANES * (6 * deep + 6 * LANES + 4 * LANES), 12 << 20),
        name=name,
    )(came, *blocks, *tables, factors)


def analyse(plan, name, joined, to, field, below, above, tables):
    count = plan.count
    tall = wire_rows(plan.rows, plan.joined - 128)
    if joined:
        shape, specs, extra = jax.ShapeDtypeStruct((count, tall, 128), F32), vmem(), []
    else:
        shape, specs = [jax.ShapeDtypeStruct((tall, 128), F32)] * count, [vmem()] * count
        extra = [pltpu.VMEM((count, tall, 128), F32)]
    return pl.pallas_call(
        functools.partial(analyse_kernel, plan, joined),
        in_specs=[smem()] + [vmem()] * 6,
        out_specs=specs,
        out_shape=shape,
        scratch_shapes=extra
        + [
            pltpu.VMEM((3 * plan.planes, LANES), BF),
            pltpu.VMEM((8 * count, LANES), F32),
            pltpu.VMEM((count, plan.rows, 128), F32),
        ],
        compiler_params=params(),
        cost_estimate=cost(3 * 2 * plan.planes * LANES * 3 * plan.planes, 6 << 20),
        name=name,
    )(to, field, below, above, *tables)


def unpack_scratch(plan, span):
    pieces = min(plan.pieces, -(-span // plan.width) + 1)
    pad = -(-plan.rows // 16) * 16
    return [pltpu.VMEM((pieces * pad, 2 * LANES), BF), pltpu.VMEM((pieces * pad, LANES), F32)]


def unpack_first(plan, gate, blocks, expand):
    out = jax.ShapeDtypeStruct((3, plan.modes, plan.nodes), F32)
    return pl.pallas_call(
        functools.partial(unpack_first_kernel, plan),
        grid=(1,),
        in_specs=[smem(), vmem(), vmem()],
        out_specs=pl.BlockSpec((3, plan.modes, plan.seam), lambda i: (0, 0, 0)),
        out_shape=out,
        scratch_shapes=unpack_scratch(plan, plan.seam),
        compiler_params=params(),
        cost_estimate=cost(2 * plan.count * plan.rows * LANES * 2 * LANES, 4 << 20),
        name="unpack_first",
    )(gate, blocks, expand)


def unpack_second(plan, came, before, old, blocks, expand):
    tall = blocks[0].shape[0]
    steps = -(-(plan.nodes - plan.seam) // plan.stride)
    skip = plan.seam // plan.stride
    return pl.pallas_call(
        functools.partial(unpack_second_kernel, plan, steps),
        grid=(steps,),
        in_specs=[
            smem(),
            pl.BlockSpec((1, tall, 128), lambda i: (plan.count - 1, 0, 0)),
            hbm(),
            pl.BlockSpec(expand.shape, lambda i: (0, 0)),
        ]
        + [pl.BlockSpec((tall, 128), lambda i: (0, 0))] * plan.count,
        out_specs=pl.BlockSpec((3, plan.modes, plan.stride), lambda i: (0, 0, i + skip)),
        out_shape=jax.ShapeDtypeStruct((3, plan.modes, plan.nodes), F32),
        scratch_shapes=[pltpu.VMEM((plan.count, tall, 128), F32)] + unpack_scratch(plan, plan.stride),
        input_output_aliases={2: 0},
        compiler_params=params(),
        cost_estimate=cost(2 * plan.count * plan.rows * LANES * 2 * LANES, 4 << 20),
        name="unpack_second",
    )(came, before, old, expand, *blocks)


def permutes(blocks, count):
    outs = [blocks[0]] + [None] * (count - 1)
    for s in sorted(range(1, count), key=lambda s: abs(2 * s - count)):
        outs[s] = lax.ppermute(blocks[s], "fourier", [(k, (k + s) % count) for k in range(count)])
    return outs


def all_at_once(blocks):
    return lax.all_to_all(blocks, "fourier", split_axis=0, concat_axis=0, tiled=True)


def rim_exchange(low, up):
    ends = lax.axis_size("elem") - 1
    below = lax.ppermute(up, "elem", [(i, i + 1) for i in range(ends)])
    above = lax.ppermute(low, "elem", [(i + 1, i) for i in range(ends)])
    return below, above


def after(x, other):
    return lax.optimization_barrier((x, other))[0]


def chunked(plan, velocity, metric, mass_weights):
    count = plan.count
    here = lax.axis_index("fourier").astype(jnp.int32)
    steps = jnp.arange(count, dtype=jnp.int32)
    to, came = (here + steps) % count, (here - steps + count) % count
    forward, forward_left, back, back_left = (jnp.asarray(t) for t in plan.tables())
    slopes = jnp.asarray(plan.slopes())
    join, rims, expand = (jnp.asarray(t) for t in plan.assembly())
    local = jnp.concatenate([metric, mass_weights[None], jnp.zeros((3, plan.nodes), F32)], axis=0)
    tables = (forward, forward_left, slopes, join)
    back_tables = (back, back_left, rims)
    factors = []
    for q in range(CHUNKS):
        start = (here + q * count) * plan.width
        cut = lax.dynamic_slice_in_dim(local, start, plan.width, 1)
        factors.append(jnp.pad(cut, ((0, 0), (0, LANES - plan.width))))

    sent = pack_first(plan, to, velocity)
    spread = permutes(sent, count)
    second = pack_second(plan, after(to, sent[1]), velocity)
    second = all_at_once(after(second, spread))
    field, low, up = synth(plan, "synth_first", came, spread, tables, factors[0])
    below, above = rim_exchange(low, up)
    back_first = analyse(plan, "analyse_first", True, to, field, below, above, back_tables)
    back_first = all_at_once(after(back_first, second))
    field, low, up = synth(plan, "synth_second", came, second, tables, factors[1])
    below, above = rim_exchange(low, up)
    back_second = analyse(plan, "analyse_second", False, to, field, below, above, back_tables)
    returned = permutes(back_second, count)
    half = unpack_first(plan, to, back_first, expand)
    return unpack_second(plan, came, back_first, half, returned, expand)


def add_shifted(field, source, reach, side):
    count = field.shape[-1]
    node = np.arange(count)
    keep = side(node) & (node + reach >= 0) & (node + reach < count)
    pads = [(0, 0)] * (field.ndim - 1)
    if reach > 0:
        moved = jnp.pad(source[..., reach:], pads + [(0, reach)])
    else:
        moved = jnp.pad(source[..., :reach], pads + [(-reach, 0)])
    return field + jnp.where(jnp.asarray(keep), moved, 0.0)


def plain(plan, velocity, metric, mass_weights):
    count, square = plan.count, NP * NP
    synthesis, spanwise, analysis = (jnp.asarray(t, F32) for t in fourier_tables(plan.planes))
    slopes = gll_diff()
    group = plan.elements // count
    eye_elem, eye_side = np.eye(group), np.eye(NP)
    xi_matrix = jnp.asarray(np.kron(eye_elem, np.kron(eye_side, slopes.T)), F32)
    eta_matrix = jnp.asarray(np.kron(eye_elem, np.kron(slopes.T, eye_side)), F32)
    spread = lax.all_to_all(velocity, "fourier", split_axis=2, concat_axis=1, tiled=True)
    offset = lax.axis_index("fourier") * group * square
    factors = lax.dynamic_slice_in_dim(metric, offset, group * square, 1)
    weights = lax.dynamic_slice_in_dim(mass_weights, offset, group * square, 0)
    values = jnp.einsum("cmn,mz->czn", spread, synthesis, precision=HIGH)
    along_z = jnp.einsum("cmn,mz->czn", spread, spanwise, precision=HIGH)
    along_xi = jnp.einsum("czk,kn->czn", values, xi_matrix, precision=HIGH)
    along_eta = jnp.einsum("czk,kn->czn", values, eta_matrix, precision=HIGH)
    grad_x = factors[0] * along_xi + factors[2] * along_eta
    grad_y = factors[1] * along_xi + factors[3] * along_eta
    weighted = weights * (values[0] * grad_x + values[1] * grad_y + values[2] * along_z)
    coeffs = jnp.einsum("czn,mz->cmn", weighted, analysis, precision=HIGH)
    coeffs = lax.all_to_all(coeffs, "fourier", split_axis=1, concat_axis=2, tiled=True)
    last = NP - 1
    reach = square - last
    joined = add_shifted(coeffs, coeffs, reach, lambda n: n % NP == last)
    joined = add_shifted(joined, coeffs, -reach, lambda n: n % NP == 0)
    below, above = rim_exchange(joined, joined)
    result = add_shifted(joined, below, last * NP, lambda n: n % square < NP)
    return add_shifted(result, above, -last * NP, lambda n: n % square >= last * NP)


def shards(velocity, metric, mass_weights):
    plan = Plan(lax.axis_size("fourier"), velocity.shape[1], velocity.shape[2])
    step = chunked if plan.fits else plain
    return step(plan, velocity, metric, mass_weights)


def solution(mesh):
    in_specs = (P(None, "fourier", "elem"), P(None, "elem"), P("elem"))
    out_specs = P(None, "fourier", "elem")
    return jax.shard_map(shards, mesh=mesh, in_specs=in_specs, out_specs=out_specs, check_vma=False)
```
